512 devices in a mesh: dom: 32 (over z, y_hi), cluster: 16 (over x, y_lo, core).
Axes of the slice: x: 4, y: 8 (y_hi: 4, y_lo: 2; y = y_hi * 2 + y_lo), z: 8, core: 2. Of those that a mesh axis runs over, the one named last changes fastest.
Arguments:
- features: bfloat16 [16, 24576, 512], P('cluster', 'dom'), may hold values from -6 to 6
- stale: bfloat16 [16, 1024, 512], P('cluster'), may hold values from -6 to 6
- boundary: int32 [16, 32], P('cluster', 'dom'), may hold values from 0 to 23
- skip: int32 [16, 32], P('cluster'), may hold values 0 or 1
- tile_vals: bfloat16 [16, 1024, 32, 128], P('cluster', 'dom'), may hold values from -0.4375 to 0.4375
- tile_row: int32 [16, 1024], P('cluster', 'dom'), may hold values from 0 to 5
- tile_src: int32 [16, 1024], P('cluster', 'dom'), may hold values from 0 to 33
- tile_count: int32 [16, 32], P('cluster', 'dom'), may hold values from 16 to 32, as said below
- weight: bfloat16 [512, 512], replicated, may hold values from -0.25 to 0.25
- cotangent: bfloat16 [16, 24576, 512], P('cluster', 'dom'), may hold values from -6 to 6
Outputs:
- out_features: bfloat16 [16, 24576, 512], P('cluster', 'dom')
- grad_features: bfloat16 [16, 24576, 512], P('cluster', 'dom')
- grad_weight: float32 [512, 512], P('dom')
The draws below stay inside these ranges and needn't reach their ends.
Inputs may be any that keep to these rules, and one draw needn't show every extreme that they name: `tile_count`: every partition has at least half of its slots live; some partition has all 32 slots live.
All inputs are finite; a program needn't handle non-finite values. No bound on the sum of `skip` on one device may be relied on, other than what follows from the above.
Results may differ from the reference program's by a relative error of at most 0.02.
Values may be sent and summed in bfloat16 or wider, within the bound.
No kernel may reach another device: no remote copies, remote signals or barrier semaphores. Data moves between devices by JAX's collectives and lax.ppermute only.
A program may use at most 64 MiB of HBM per device.

```python
import jax
import jax.numpy as jnp
from jax import lax

F = 512
NODE_DEV = 768
BLK = 32
TR = 128
TPD = 32
GROUP_NODES = 24576
CACHE_ROWS = 1024
N_DOM = 32
N_CLUSTER = 16


def draw_tile_count(key, part):
    first = jax.random.fold_in(key, 11)
    second = jax.random.fold_in(key, 23)
    third = jax.random.fold_in(key, 37)
    shape = (N_CLUSTER, N_DOM)
    base = jax.random.randint(first, shape, TPD // 2, TPD + 1)
    heavy = jax.random.randint(second, shape, 0, 8) == 0
    counts = jnp.where(heavy, TPD, base)
    where_full = jax.random.randint(third, (), 0, N_CLUSTER * N_DOM)
    flat = counts.reshape(-1)
    flat = jnp.where(jnp.arange(N_CLUSTER * N_DOM) == where_full, TPD, flat)
    return flat.reshape(shape).astype(jnp.int32)


def set_ends(array, rng, low, top_value):
    place = [jax.random.randint(jax.random.fold_in(rng, axis), (), 0, length) for axis, length in enumerate(array.shape)]
    main_axis = array.shape.index(max(array.shape))
    neighbour = place[:main_axis] + [(place[main_axis] + 1) % array.shape[main_axis]] + place[main_axis + 1:]
    return array.at[tuple(place)].set(low).at[tuple(neighbour)].set(top_value)


def block_levels(key, dims, cuts, low, top_value):
    level = 1.0
    for axis_at, shards_of in cuts:
        steps = jax.random.uniform(jax.random.fold_in(jax.random.fold_in(key, 6), axis_at), (shards_of,), jnp.float32, low / len(cuts), top_value / len(cuts))
        level = level * jnp.repeat(jnp.exp(steps), dims[axis_at] // shards_of).reshape((-1,) + (1,) * (len(dims) - 1 - axis_at))
    return level


def centred(stream_key, extent, scale, bound, cuts=(), kind=jnp.bfloat16):
    array = scale * jax.random.normal(stream_key, extent, jnp.float32)
    if cuts:
        array = array * block_levels(stream_key, extent, cuts, -0.22, 0.18)
    return jnp.clip(array, -bound, bound).astype(kind)


def setup_inputs(seed: int = 0) -> dict:
    splits = jax.random.split(jax.random.key(seed), 11)
    features = centred(splits[0], (N_CLUSTER, GROUP_NODES, F), 1.0, 6.0, ((0, 16), (1, 32)))
    stale = centred(splits[1], (N_CLUSTER, CACHE_ROWS, F), 1.0, 6.0, ((0, 16),))
    boundary = set_ends(jax.random.randint(splits[2], (N_CLUSTER, N_DOM), 0, NODE_DEV // BLK), jax.random.fold_in(splits[2], 1), 0, (NODE_DEV // BLK) - 1).astype(jnp.int32)
    skip = set_ends((jax.random.randint(splits[3], (N_CLUSTER, N_DOM), 0, 4) < 1).astype(jnp.int32), jax.random.fold_in(splits[3], 1), 0, 1)
    tile_vals = centred(splits[4], (N_CLUSTER, N_DOM * TPD, BLK, TR), (BLK * TPD * TR // NODE_DEV) ** -0.5, 0.4375, ((0, 16), (1, 32)))
    tile_row = set_ends(jax.random.randint(splits[5], (N_CLUSTER, N_DOM * TPD), 0, NODE_DEV // TR), jax.random.fold_in(splits[5], 1), 0, (NODE_DEV // TR) - 1).astype(jnp.int32)
    tile_src = set_ends(jax.random.randint(splits[6], (N_CLUSTER, N_DOM * TPD), 0, N_DOM + 2), jax.random.fold_in(splits[6], 1), 0, (N_DOM + 2) - 1).astype(jnp.int32)
    tile_count = draw_tile_count(jax.random.fold_in(splits[10], 71), 0)
    weight = centred(splits[8], (F, F), F ** -0.5, 0.25)
    cotangent = centred(splits[9], (N_CLUSTER, GROUP_NODES, F), 1.0, 6.0, ((0, 16), (1, 32)))
    return dict(features=features, stale=stale, boundary=boundary, skip=skip, tile_vals=tile_vals, tile_row=tile_row, tile_src=tile_src, tile_count=tile_count, weight=weight, cotangent=cotangent)


def silu_parts(value):
    sig = jax.nn.sigmoid(value)
    return value * sig, sig * (1.0 + value * (1.0 - sig))


def reference(features, stale, boundary, skip, tile_vals, tile_row, tile_src, tile_count, weight, cotangent):
    n_clu = N_CLUSTER
    n_part = N_DOM
    n_blocks = NODE_DEV // BLK
    n_rowblk = NODE_DEV // TR
    blocks = features.reshape(n_clu, n_part, n_blocks, BLK, F)
    picks = boundary.astype(jnp.int32)[:, :, None, None, None]
    exported = jnp.take_along_axis(blocks, picks, axis=2)[:, :, 0]
    cached = stale.reshape(n_clu, n_part, BLK, F)
    fresh = jnp.where((skip == 1)[:, :, None, None], cached, exported)
    lower = jnp.roll(exported, 1, axis=0)
    upper = jnp.roll(exported, -1, axis=0)
    tile_blocks = tile_vals.reshape(n_clu * n_part, TPD, BLK, TR)
    rows = tile_row.reshape(n_clu * n_part, TPD)
    srcs = tile_src.reshape(n_clu * n_part, TPD)
    counts = tile_count.reshape(n_clu * n_part)
    feats = features.reshape(n_clu * n_part, NODE_DEV, F)
    cots = cotangent.reshape(n_clu * n_part, NODE_DEV, F)

    def visit(carry, index):
        wsum, gsum = carry
        clu = index // n_part
        part = index % n_part
        table = jnp.concatenate([fresh[clu], lower[clu, part][None], upper[clu, part][None]], axis=0)
        active_mask = (jnp.arange(TPD, dtype=jnp.int32) < counts[index]).astype(jnp.float32)
        local_tile_block = tile_blocks[index].astype(jnp.float32)
        selected_block = jnp.take(table, srcs[index], axis=0).astype(jnp.float32)
        contribution = jnp.einsum("wnz,wnx->wzx", local_tile_block, selected_block) * active_mask[:, None, None]
        row_onehot_mask = (rows[index][:, None] == jnp.arange(n_rowblk, dtype=jnp.int32)[None, :]).astype(jnp.float32)
        row_onehot_mask = row_onehot_mask * active_mask[:, None]
        aggregate_block_list = jnp.einsum("xn,xij->nij", row_onehot_mask, contribution, precision=lax.Precision.HIGHEST)
        agg = (feats[index].astype(jnp.float32) + aggregate_block_list.reshape(NODE_DEV, F)).astype(jnp.bfloat16)
        zval = jnp.dot(agg, weight, preferred_element_type=jnp.float32)
        act, slope = silu_parts(zval)
        dz = (cots[index].astype(jnp.float32) * slope).astype(jnp.bfloat16)
        wsum = wsum + lax.dot_general(agg, dz, (((0,), (0,)), ((), ())), preferred_element_type=jnp.float32)
        dagg = lax.dot_general(dz, weight, (((1,), (1,)), ((), ())), preferred_element_type=jnp.float32).astype(jnp.bfloat16)
        selected_rows = jnp.take(dagg.reshape(n_rowblk, TR, F), rows[index], axis=0).astype(jnp.float32)
        selected_gradient = jnp.einsum("dck,dkn->dcn", local_tile_block, selected_rows) * active_mask[:, None, None]
        src_hot = (srcs[index][:, None] == jnp.arange(n_part + 2, dtype=jnp.int32)[None, :]).astype(jnp.float32)
        dsrc = jnp.einsum("ts,tbf->sbf", src_hot, selected_gradient, precision=lax.Precision.HIGHEST)
        keep = (1 - skip[clu]).astype(jnp.float32)
        gsum = gsum.at[clu].add(dsrc[:n_part] * keep[:, None, None])
        return (wsum, gsum), (act.astype(jnp.bfloat16), dagg, dsrc[n_part], dsrc[n_part + 1])

    init = (jnp.zeros((F, F), jnp.float32), jnp.zeros((n_clu, n_part, BLK, F), jnp.float32))
    (wsum, gsum), (outs, daggs, low_grads, up_grads) = lax.scan(visit, init, jnp.arange(n_clu * n_part, dtype=jnp.int32))
    low_grads = low_grads.reshape(n_clu, n_part, BLK, F)
    up_grads = up_grads.reshape(n_clu, n_part, BLK, F)
    bgrad = gsum + jnp.roll(low_grads, -1, axis=0) + jnp.roll(up_grads, 1, axis=0)
    hot = (boundary[:, :, None] == jnp.arange(n_blocks, dtype=jnp.int32)[None, None, :]).astype(jnp.float32)
    full = daggs.reshape(n_clu, n_part, n_blocks, BLK, F).astype(jnp.float32)
    full = full + hot[:, :, :, None, None] * bgrad[:, :, None]
    out_features = outs.reshape(n_clu, n_part * NODE_DEV, F)
    grad_features = full.reshape(n_clu, n_part * NODE_DEV, F).astype(jnp.bfloat16)
    return out_features, grad_features, wsum
```

```python
import jax
import jax.numpy as jnp
from jax import lax
from jax.experimental import pallas as pl
from jax.experimental.pallas import tpu as pltpu
from jax.sharding import Mesh
from jax.sharding import PartitionSpec as P

Z, YH = 8, 4
DOM = ("dom_0", "dom_1")
ALL = ("dom_0", "dom_1", "cluster")
f32 = jnp.float32
bf16 = jnp.bfloat16


def groups(clusters):
    at = lambda z, y, c: (z * YH + y) * clusters + c
    eights, fours = [], []
    for c in range(clusters):
        if c % 2 == 0:
            eights += [[at(z, y, c) for z in range(Z)] for y in range(YH)]
            fours += [[at(z, y, c) for y in range(YH)] for z in range(Z)]
        else:
            eights += [
                [at(2 * h + b, y, c) for b in range(2) for y in range(YH)] for h in range(Z // 2)
            ]
            fours += [
                [at(2 * h + b, y, c) for h in range(Z // 2)] for b in range(2) for y in range(YH)
            ]
    return eights, fours


def exchange(x, grouping):
    return lax.all_to_all(x, ALL, 0, 0, axis_index_groups=grouping, tiled=True)


def for_each(x, count):
    return jnp.broadcast_to(x, (count, *x.shape))


def passed_along(x, axis, by):
    count = lax.axis_size(axis)
    return lax.ppermute(x, axis, [(i, (i + by) % count) for i in range(count)])


def place_of(part, odd):
    z, y = part // YH, part % YH
    return jnp.where(odd == 1, (z % 2) * (Z // 2 * YH) + y * (Z // 2) + z // 2, part)


def before_kernel(
    src_ref, row_ref, count_ref, skip_ref, odd_ref, tiles_ref, feats_ref, stale_ref, lower_ref,
    upper_ref, base_ref, p_ref, pt_ref, ptn_ref, acc_ref,
):
    slots, blk, tr = tiles_ref.shape
    parts = skip_ref.shape[1]
    cached = parts * blk
    near = cached + 2 * blk
    total = near + cached
    acc_ref[...] = jnp.zeros_like(acc_ref)
    count = count_ref[0, 0]
    odd = odd_ref[0]

    def add_tile(t, carry):
        @pl.when(t < count)
        def _():
            s = src_ref[0, t]
            inside = jnp.minimum(s, parts - 1)
            sent = jnp.logical_and(s < parts, skip_ref[0, inside] != 1)
            block = jnp.where(sent, parts + 2 + place_of(inside, odd), s)
            rows = pl.ds(pl.multiple_of(block * blk, blk), blk)
            r = row_ref[0, t]
            acc_ref[r, rows, :] += tiles_ref[t].astype(f32)

        return carry

    lax.fori_loop(0, slots, add_tile, 0)
    near_rows = jnp.concatenate([lower_ref[...], upper_ref[...]], axis=0)
    for r in range(acc_ref.shape[0]):
        out = slice(r * tr, (r + 1) * tr)
        old = acc_ref[r, :cached, :].T.astype(bf16)
        beside = acc_ref[r, cached:near, :].astype(bf16)
        part = jnp.dot(old, stale_ref[...], preferred_element_type=f32)
        part += lax.dot_general(
            beside, near_rows, (((0,), (0,)), ((), ())), preferred_element_type=f32
        )
        base_ref[out, :] = feats_ref[out, :].astype(f32) + part
        new = acc_ref[r, near:total, :]
        p_ref[out, :] = new.T.astype(bf16)
        pt_ref[:, out] = new.astype(bf16)
        ptn_ref[:, out] = beside


def after_kernel(
    odd_ref, base_ref, p_ref, table_ref, weight_ref, cot_ref, pt_ref, ptn_ref,
    out_ref, dagg_ref, send_ref, near_ref, agg_ref, dz_ref,
):
    nodes, width = cot_ref.shape
    parts = send_ref.shape[0]
    blk = near_ref.shape[1]
    share = send_ref.shape[1] - blk
    step = 256
    for i in range(nodes // step):
        rows = slice(i * step, (i + 1) * step)
        agg = base_ref[rows, :] + jnp.dot(
            p_ref[rows, :], table_ref[...], preferred_element_type=f32
        )
        agg = agg.astype(bf16)
        agg_ref[rows, :] = agg
        z = jnp.dot(agg, weight_ref[...], preferred_element_type=f32)
        sig = jax.nn.sigmoid(z)
        out_ref[rows, :] = (z * sig).astype(bf16)
        slope = sig * (1.0 + z * (1.0 - sig))
        dz = (cot_ref[rows, :].astype(f32) * slope).astype(bf16)
        dz_ref[rows, :] = dz
        dagg_ref[rows, :] = lax.dot_general(
            dz, weight_ref[...], (((1,), (1,)), ((), ())), preferred_element_type=f32
        ).astype(bf16)
    odd = odd_ref[0]
    for i in range(width // 256):
        cols = slice(i * 256, (i + 1) * 256)
        gw = lax.dot_general(
            agg_ref[:, cols], dz_ref[...], (((0,), (0,)), ((), ())), preferred_element_type=f32
        ).astype(bf16)
        per = 256 // share
        for j in range(per):
            place = place_of(jnp.int32(i * per + j), odd)
            send_ref[place, blk:, :] = gw[j * share : (j + 1) * share, :]
    for i in range(parts * blk // step):
        rows = slice(i * step, (i + 1) * step)
        d = jnp.dot(pt_ref[rows, :], dagg_ref[...], preferred_element_type=f32).astype(bf16)
        per = step // blk
        send_ref[i * per : (i + 1) * per, :blk, :] = d.reshape(per, blk, width)
    d = jnp.dot(ptn_ref[...], dagg_ref[...], preferred_element_type=f32).astype(bf16)
    near_ref[...] = d.reshape(2, blk, width)


def per_device(
    features, stale, boundary, skip, tile_vals, tile_row, tile_src, tile_count, weight, cotangent
):
    feats = features[0]
    nodes, width = feats.shape
    parts = lax.axis_size(DOM)
    clusters = lax.axis_size("cluster")
    blk = stale.shape[1] // parts
    slots, _, tr = tile_vals.shape[1:]
    row_blocks = nodes // tr
    share = width // parts
    eights, fours = groups(clusters)
    odd = (lax.axis_index("cluster") % 2).astype(jnp.int32).reshape(1)
    start_row = boundary[0, 0] * blk
    own = lax.dynamic_slice_in_dim(feats, start_row, blk, 0)
    some = exchange(for_each(own, YH), fours).reshape(YH * blk, width)
    lower = passed_along(own, "cluster", 1)
    upper = passed_along(own, "cluster", -1)
    smem = pl.BlockSpec(memory_space=pltpu.SMEM)
    vmem = pl.BlockSpec(memory_space=pltpu.VMEM)
    base, p, pt, ptn = pl.pallas_call(
        before_kernel,
        out_shape=(
            jax.ShapeDtypeStruct((nodes, width), f32),
            jax.ShapeDtypeStruct((nodes, parts * blk), bf16),
            jax.ShapeDtypeStruct((parts * blk, nodes), bf16),
            jax.ShapeDtypeStruct((2 * blk, nodes), bf16),
        ),
        in_specs=[smem] * 5 + [vmem] * 5,
        out_specs=(vmem,) * 4,
        scratch_shapes=[pltpu.VMEM((row_blocks, (2 * parts + 2) * blk, tr), f32)],
        compiler_params=pltpu.CompilerParams(vmem_limit_bytes=24 << 20),
        cost_estimate=pl.CostEstimate(
            flops=2 * nodes * width * (parts + 2) * blk, bytes_accessed=8 << 20, transcendentals=0
        ),
        name="before",
    )(tile_src, tile_row, tile_count, skip, odd, tile_vals[0], feats, stale[0], lower, upper)
    table = exchange(for_each(some, Z), eights).reshape(parts * blk, width)
    out_features, dagg, send, near = pl.pallas_call(
        after_kernel,
        out_shape=(
            jax.ShapeDtypeStruct((nodes, width), bf16),
            jax.ShapeDtypeStruct((nodes, width), bf16),
            jax.ShapeDtypeStruct((parts, blk + share, width), bf16),
            jax.ShapeDtypeStruct((2, blk, width), bf16),
        ),
        in_specs=[smem] + [vmem] * 7,
        out_specs=(vmem,) * 4,
        scratch_shapes=[pltpu.VMEM((nodes, width), bf16), pltpu.VMEM((nodes, width), bf16)],
        compiler_params=pltpu.CompilerParams(vmem_limit_bytes=24 << 20),
        cost_estimate=pl.CostEstimate(
            flops=2 * nodes * width * (3 * width + 2 * (parts + 1) * blk),
            bytes_accessed=11 << 20,
            transcendentals=nodes * width,
        ),
        name="after",
    )(odd, base, p, table, weight, cotangent[0], pt, ptn)
    rows = blk + share
    got = exchange(send.reshape(Z, YH * rows, width), eights)
    from_upper = passed_along(near[0], "cluster", -1)
    from_lower = passed_along(near[1], "cluster", 1)
    some = got.astype(f32).sum(axis=0).astype(bf16)
    got = exchange(some.reshape(YH, rows, width), fours)
    mine = got.astype(f32).sum(axis=0)
    gw = lax.all_to_all(for_each(mine[blk:].astype(bf16), clusters), "cluster", 0, 0, tiled=True)
    grad_weight = gw.astype(f32).sum(axis=0)
    bgrad = mine[:blk] + from_upper.astype(f32) + from_lower.astype(f32)
    current = lax.dynamic_slice_in_dim(dagg, start_row, blk, 0).astype(f32)
    grad_features = lax.dynamic_update_slice_in_dim(
        dagg, (current + bgrad).astype(bf16), start_row, 0
    )
    return (out_features[None], grad_features[None], grad_weight)


def solution(mesh):
    finer = Mesh(mesh.devices.reshape(Z, YH, mesh.shape["cluster"]), ALL)
    placed = (
        P("cluster", DOM, None),
        P("cluster", None, None),
        P("cluster", DOM),
        P("cluster", None),
        P("cluster", DOM, None, None),
        P("cluster", DOM),
        P("cluster", DOM),
        P("cluster", DOM),
        P(),
        P("cluster", DOM, None),
    )
    return jax.shard_map(
        per_device,
        mesh=finer,
        in_specs=placed,
        out_specs=(P("cluster", DOM, None), P("cluster", DOM, None), P(DOM, None)),
        check_vma=False,
    )
```

```python
import jax
import jax.numpy as jnp
from jax import lax
from jax.experimental import pallas as pl
from jax.experimental.pallas import tpu as pltpu
from jax.sharding import Mesh
from jax.sharding import PartitionSpec as P

Z, YH = 8, 4
DOM = ("dom_0", "dom_1")
ALL = ("dom_0", "dom_1", "cluster")
f32 = jnp.float32
bf16 = jnp.bfloat16


def groups(clusters):
    at = lambda z, y, c: (z * YH + y) * clusters + c
    eights, fours = [], []
    for c in range(clusters):
        if c % 2 == 0:
            eights += [[at(z, y, c) for z in range(Z)] for y in range(YH)]
            fours += [[at(z, y, c) for y in range(YH)] for z in range(Z)]
        else:
            eights += [
                [at(2 * h + b, y, c) for b in range(2) for y in range(YH)] for h in range(Z // 2)
            ]
            fours += [
                [at(2 * h + b, y, c) for h in range(Z // 2)] for b in range(2) for y in range(YH)
            ]
    return eights, fours


def exchange(x, grouping):
    return lax.all_to_all(x, ALL, 0, 0, axis_index_groups=grouping, tiled=True)


def for_each(x, count):
    return jnp.broadcast_to(x, (count, *x.shape))


def passed_along(x, axis, by):
    count = lax.axis_size(axis)
    return lax.ppermute(x, axis, [(i, (i + by) % count) for i in range(count)])


def place_of(part, odd):
    z, y = part // YH, part % YH
    return jnp.where(odd == 1, (z % 2) * (Z // 2 * YH) + y * (Z // 2) + z // 2, part)


def before_kernel(
    src_ref, row_ref, count_ref, skip_ref, odd_ref, tiles_ref, feats_ref, stale_ref,
    base_ref, p_ref, pt_ref, ptn_ref, pn_ref, acc_ref,
):
    slots, blk, tr = tiles_ref.shape
    parts = skip_ref.shape[1]
    cached = parts * blk
    near = cached + 2 * blk
    acc_ref[...] = jnp.zeros_like(acc_ref)
    count = count_ref[0, 0]
    odd = odd_ref[0]

    def add_tile(t, carry):
        @pl.when(t < count)
        def _():
            s = src_ref[0, t]
            inside = jnp.minimum(s, parts - 1)
            sent = jnp.logical_and(s < parts, skip_ref[0, inside] != 1)
            block = jnp.where(sent, parts + 2 + place_of(inside, odd), s)
            rows = pl.ds(pl.multiple_of(block * blk, blk), blk)
            r = row_ref[0, t]
            acc_ref[r, rows, :] += tiles_ref[t].astype(f32)

        return carry

    lax.fori_loop(0, slots, add_tile, 0)
    for r in range(acc_ref.shape[0]):
        out = slice(r * tr, (r + 1) * tr)
        old = acc_ref[r, :cached, :].T.astype(bf16)
        base_ref[out, :] = feats_ref[out, :].astype(f32) + jnp.dot(
            old, stale_ref[...], preferred_element_type=f32
        )
        beside = acc_ref[r, cached:near, :]
        pn_ref[out, :] = beside.T.astype(bf16)
        ptn_ref[:, out] = beside.astype(bf16)
        new = acc_ref[r, near:, :]
        p_ref[out, :] = new.T.astype(bf16)
        pt_ref[:, out] = new.astype(bf16)


def after_kernel(
    odd_ref, base_hbm, p_hbm, cot_hbm, weight_hbm, ptn_hbm, pt_hbm, pn_ref, table_ref, lower_ref,
    upper_ref, out_hbm, dagg_ref, send_ref, near_ref,
    base_ref, p_ref, cot_ref, weight_ref, ptn_ref, pt_ref, out_ref, agg_ref, dz_ref, sems, out_sems,
):
    nodes, width = cot_ref.shape
    parts = send_ref.shape[0]
    blk = near_ref.shape[1]
    share = send_ref.shape[1] - blk
    step = 256
    steps = nodes // step
    chunk = lambda i: slice(i * step, (i + 1) * step)

    def fetch(source, target, rows, sem):
        copy = pltpu.make_async_copy(source.at[rows, :], target.at[rows, :], sems.at[sem])
        copy.start()
        return copy

    whole = slice(None)
    arriving = []
    for i in range(steps):
        rows = chunk(i)
        ahead = [fetch(p_hbm, p_ref, rows, 3 * i), fetch(base_hbm, base_ref, rows, 3 * i + 1)]
        if i == 0:
            of_weight = fetch(weight_hbm, weight_ref, whole, 3 * steps)
        ahead.append(fetch(cot_hbm, cot_ref, rows, 3 * i + 2))
        arriving.append(ahead)
    late = [
        fetch(ptn_hbm, ptn_ref, whole, 3 * steps + 1), fetch(pt_hbm, pt_ref, whole, 3 * steps + 2)
    ]
    near_rows = jnp.concatenate([lower_ref[...], upper_ref[...]], axis=0)
    leaving = []
    for i in range(steps):
        rows = chunk(i)
        of_p, of_base, of_cot = arriving[i]
        of_p.wait()
        new = jnp.dot(p_ref[rows, :], table_ref[...], preferred_element_type=f32)
        new += jnp.dot(pn_ref[rows, :], near_rows, preferred_element_type=f32)
        of_base.wait()
        agg = (base_ref[rows, :] + new).astype(bf16)
        agg_ref[rows, :] = agg
        if i == 0:
            of_weight.wait()
        z = jnp.dot(agg, weight_ref[...], preferred_element_type=f32)
        sig = jax.nn.sigmoid(z)
        out_ref[rows, :] = (z * sig).astype(bf16)
        copy = pltpu.make_async_copy(out_ref.at[rows, :], out_hbm.at[rows, :], out_sems.at[i])
        copy.start()
        leaving.append(copy)
        slope = sig * (1.0 + z * (1.0 - sig))
        of_cot.wait()
        dz = (cot_ref[rows, :].astype(f32) * slope).astype(bf16)
        dz_ref[rows, :] = dz
        dagg_ref[rows, :] = lax.dot_general(
            dz, weight_ref[...], (((1,), (1,)), ((), ())), preferred_element_type=f32
        ).astype(bf16)
    odd = odd_ref[0]
    for i in range(width // step):
        gw = lax.dot_general(
            agg_ref[:, chunk(i)], dz_ref[...], (((0,), (0,)), ((), ())), preferred_element_type=f32
        ).astype(bf16)
        per = step // share
        for j in range(per):
            place = place_of(jnp.int32(i * per + j), odd)
            send_ref[place, blk:, :] = gw[j * share : (j + 1) * share, :]
    for copy in late:
        copy.wait()
    for i in range(parts * blk // step):
        d = jnp.dot(pt_ref[chunk(i), :], dagg_ref[...], preferred_element_type=f32).astype(bf16)
        per = step // blk
        send_ref[i * per : (i + 1) * per, :blk, :] = d.reshape(per, blk, width)
    d = jnp.dot(ptn_ref[...], dagg_ref[...], preferred_element_type=f32).astype(bf16)
    near_ref[...] = d.reshape(2, blk, width)
    for copy in leaving:
        copy.wait()


def per_device(
    features, stale, boundary, skip, tile_vals, tile_row, tile_src, tile_count, weight, cotangent
):
    feats = features[0]
    nodes, width = feats.shape
    parts = lax.axis_size(DOM)
    clusters = lax.axis_size("cluster")
    blk = stale.shape[1] // parts
    slots, _, tr = tile_vals.shape[1:]
    row_blocks = nodes // tr
    share = width // parts
    eights, fours = groups(clusters)
    odd = (lax.axis_index("cluster") % 2).astype(jnp.int32).reshape(1)
    start_row = boundary[0, 0] * blk
    own = lax.dynamic_slice_in_dim(feats, start_row, blk, 0)
    some = exchange(for_each(own, YH), fours).reshape(YH * blk, width)
    lower = passed_along(own, "cluster", 1)
    upper = passed_along(own, "cluster", -1)
    smem = pl.BlockSpec(memory_space=pltpu.SMEM)
    vmem = pl.BlockSpec(memory_space=pltpu.VMEM)
    hbm = pl.BlockSpec(memory_space=pltpu.HBM)
    base, p, pt, ptn, pn = pl.pallas_call(
        before_kernel,
        out_shape=(
            jax.ShapeDtypeStruct((nodes, width), f32),
            jax.ShapeDtypeStruct((nodes, parts * blk), bf16),
            jax.ShapeDtypeStruct((parts * blk, nodes), bf16),
            jax.ShapeDtypeStruct((2 * blk, nodes), bf16),
            jax.ShapeDtypeStruct((nodes, 2 * blk), bf16),
        ),
        in_specs=[smem] * 5 + [vmem] * 3,
        out_specs=(vmem,) * 5,
        scratch_shapes=[pltpu.VMEM((row_blocks, (2 * parts + 2) * blk, tr), f32)],
        compiler_params=pltpu.CompilerParams(vmem_limit_bytes=60 << 20),
        cost_estimate=pl.CostEstimate(
            flops=2 * nodes * width * parts * blk, bytes_accessed=8 << 20, transcendentals=0
        ),
        name="before",
    )(tile_src, tile_row, tile_count, skip, odd, tile_vals[0], feats, stale[0])
    table = exchange(for_each(some, Z), eights).reshape(parts * blk, width)
    out_features, dagg, send, near = pl.pallas_call(
        after_kernel,
        out_shape=(
            jax.ShapeDtypeStruct((nodes, width), bf16),
            jax.ShapeDtypeStruct((nodes, width), bf16),
            jax.ShapeDtypeStruct((parts, blk + share, width), bf16),
            jax.ShapeDtypeStruct((2, blk, width), bf16),
        ),
        in_specs=[smem] + [hbm] * 6 + [vmem] * 4,
        out_specs=(hbm, vmem, vmem, vmem),
        scratch_shapes=[
            pltpu.VMEM((nodes, width), f32),
            pltpu.VMEM((nodes, parts * blk), bf16),
            pltpu.VMEM((nodes, width), bf16),
            pltpu.VMEM((width, width), bf16),
            pltpu.VMEM((2 * blk, nodes), bf16),
            pltpu.VMEM((parts * blk, nodes), bf16),
            pltpu.VMEM((nodes, width), bf16),
            pltpu.VMEM((nodes, width), bf16),
            pltpu.VMEM((nodes, width), bf16),
            pltpu.SemaphoreType.DMA((nodes // 256 * 3 + 3,)),
            pltpu.SemaphoreType.DMA((nodes // 256,)),
        ],
        compiler_params=pltpu.CompilerParams(vmem_limit_bytes=48 << 20),
        cost_estimate=pl.CostEstimate(
            flops=2 * nodes * width * (3 * width + 2 * (parts + 1) * blk),
            bytes_accessed=11 << 20,
            transcendentals=nodes * width,
        ),
        name="after",
    )(odd, base, p, cotangent[0], weight, ptn, pt, pn, table, lower, upper)
    rows = blk + share
    got = exchange(send.reshape(Z, YH * rows, width), eights)
    from_upper = passed_along(near[0], "cluster", -1)
    from_lower = passed_along(near[1], "cluster", 1)
    some = got.astype(f32).sum(axis=0).astype(bf16)
    some, from_upper, from_lower = lax.optimization_barrier((some, from_upper, from_lower))
    got = exchange(some.reshape(YH, rows, width), fours)
    mine = got.astype(f32).sum(axis=0)
    gw = lax.all_to_all(for_each(mine[blk:].astype(bf16), clusters), "cluster", 0, 0, tiled=True)
    grad_weight = gw.astype(f32).sum(axis=0)
    bgrad = mine[:blk] + from_upper.astype(f32) + from_lower.astype(f32)
    current = lax.dynamic_slice_in_dim(dagg, start_row, blk, 0).astype(f32)
    grad_features = lax.dynamic_update_slice_in_dim(
        dagg, (current + bgrad).astype(bf16), start_row, 0
    )
    return (out_features[None], grad_features[None], grad_weight)


def solution(mesh):
    finer = Mesh(mesh.devices.reshape(Z, YH, mesh.shape["cluster"]), ALL)
    placed = (
        P("cluster", DOM, None),
        P("cluster", None, None),
        P("cluster", DOM),
        P("cluster", None),
        P("cluster", DOM, None, None),
        P("cluster", DOM),
        P("cluster", DOM),
        P("cluster", DOM),
        P(),
        P("cluster", DOM, None),
    )
    return jax.shard_map(
        per_device,
        mesh=finer,
        in_specs=placed,
        out_specs=(P("cluster", DOM, None), P("cluster", DOM, None), P(DOM, None)),
        check_vma=False,
    )
```

```python
import jax
import jax.numpy as jnp
from jax import lax
from jax.experimental import pallas as pl
from jax.experimental.pallas import tpu as pltpu
from jax.sharding import Mesh
from jax.sharding import PartitionSpec as P

Z, YH = 8, 4
DOM = ("dom_0", "dom_1")
ALL = ("dom_0", "dom_1", "cluster")
f32 = jnp.float32
bf16 = jnp.bfloat16


def groups(clusters):
    at = lambda z, y, c: (z * YH + y) * clusters + c
    eights, fours = [], []
    for c in range(clusters):
        if c % 2 == 0:
            eights += [[at(z, y, c) for z in range(Z)] for y in range(YH)]
            fours += [[at(z, y, c) for y in range(YH)] for z in range(Z)]
        else:
            eights += [
                [at(2 * h + b, y, c) for b in range(2) for y in range(YH)] for h in range(Z // 2)
            ]
            fours += [
                [at(2 * h + b, y, c) for h in range(Z // 2)] for b in range(2) for y in range(YH)
            ]
    return eights, fours


def exchange(x, grouping):
    return lax.all_to_all(x, ALL, 0, 0, axis_index_groups=grouping, tiled=True)


def for_each(x, count):
    return jnp.broadcast_to(x, (count, *x.shape))


def passed_along(x, axis, by):
    count = lax.axis_size(axis)
    return lax.ppermute(x, axis, [(i, (i + by) % count) for i in range(count)])


def place_of(part, odd):
    return jnp.where(odd == 1, part, part % YH * Z + part // YH)


def before_kernel(
    src_ref, row_ref, count_ref, skip_ref, odd_ref, tiles_ref, feats_ref, stale_ref,
    base_ref, p_ref, pt_ref, acc_ref,
):
    slots, blk, tr = tiles_ref.shape
    parts = skip_ref.shape[1]
    cached = parts * blk
    acc_ref[...] = jnp.zeros_like(acc_ref)
    count = count_ref[0, 0]
    odd = odd_ref[0]

    def add_tile(t, carry):
        @pl.when(t < count)
        def _():
            s = src_ref[0, t]
            inside = jnp.minimum(s, parts - 1)
            kept = jnp.logical_and(s < parts, skip_ref[0, inside] == 1)
            sent = parts + jnp.where(s < parts, place_of(inside, odd), s)
            block = jnp.where(kept, s, sent)
            rows = pl.ds(pl.multiple_of(block * blk, blk), blk)
            r = row_ref[0, t]
            acc_ref[r, rows, :] += tiles_ref[t].astype(f32)

        return carry

    lax.fori_loop(0, slots, add_tile, 0)
    live = pt_ref.shape[0]
    for r in range(acc_ref.shape[0]):
        out = slice(r * tr, (r + 1) * tr)
        old = acc_ref[r, :cached, :].T.astype(bf16)
        base_ref[out, :] = feats_ref[out, :].astype(f32) + jnp.dot(
            old, stale_ref[...], preferred_element_type=f32
        )
        new = acc_ref[r, cached:, :]
        p_ref[out, :] = new.T.astype(bf16)
        pt_ref[:, out] = new[:live, :].astype(bf16)


def after_kernel(
    odd_ref, base_hbm, p_hbm, cot_hbm, weight_hbm, pt_hbm, table_ref, lower_ref, upper_ref,
    out_hbm, dagg_ref, send_hbm, near_ref,
    base_ref, p_ref, cot_ref, weight_ref, pt_ref, out_ref, send_ref, agg_ref, dz_ref, sems,
    out_sems, send_sems,
):
    nodes, width = cot_ref.shape
    parts = send_ref.shape[0]
    blk = near_ref.shape[1]
    share = send_ref.shape[1] - blk
    step = 256
    steps = nodes // step
    chunk = lambda i: slice(i * step, (i + 1) * step)

    def fetch(source, target, rows, sem):
        copy = pltpu.make_async_copy(source.at[rows, :], target.at[rows, :], sems.at[sem])
        copy.start()
        return copy

    whole = slice(None)
    arriving = []
    for i in range(steps):
        rows = chunk(i)
        ahead = [fetch(p_hbm, p_ref, rows, 3 * i), fetch(base_hbm, base_ref, rows, 3 * i + 1)]
        if i == 0:
            of_weight = fetch(weight_hbm, weight_ref, whole, 3 * steps)
        ahead.append(fetch(cot_hbm, cot_ref, rows, 3 * i + 2))
        arriving.append(ahead)
    of_pt = fetch(pt_hbm, pt_ref, whole, 3 * steps + 1)
    cached = parts * blk
    near_rows = jnp.concatenate([lower_ref[...], upper_ref[...]], axis=0)
    leaving = []
    for i in range(steps):
        rows = chunk(i)
        of_p, of_base, of_cot = arriving[i]
        of_p.wait()
        new = jnp.dot(p_ref[rows, :cached], table_ref[...], preferred_element_type=f32)
        new += jnp.dot(
            p_ref[rows, cached : cached + 2 * blk], near_rows, preferred_element_type=f32
        )
        of_base.wait()
        agg = (base_ref[rows, :] + new).astype(bf16)
        agg_ref[rows, :] = agg
        if i == 0:
            of_weight.wait()
        z = jnp.dot(agg, weight_ref[...], preferred_element_type=f32)
        sig = jax.nn.sigmoid(z)
        out_ref[rows, :] = (z * sig).astype(bf16)
        copy = pltpu.make_async_copy(out_ref.at[rows, :], out_hbm.at[rows, :], out_sems.at[i])
        copy.start()
        leaving.append(copy)
        slope = sig * (1.0 + z * (1.0 - sig))
        of_cot.wait()
        dz = (cot_ref[rows, :].astype(f32) * slope).astype(bf16)
        dz_ref[rows, :] = dz
        dagg_ref[rows, :] = lax.dot_general(
            dz, weight_ref[...], (((1,), (1,)), ((), ())), preferred_element_type=f32
        ).astype(bf16)
    odd = odd_ref[0]
    for i in range(width // step):
        gw = lax.dot_general(
            agg_ref[:, chunk(i)], dz_ref[...], (((0,), (0,)), ((), ())), preferred_element_type=f32
        ).astype(bf16)
        per = step // share
        for j in range(per):
            place = place_of(jnp.int32(i * per + j), odd)
            send_ref[place, blk:, :] = gw[j * share : (j + 1) * share, :]
    of_pt.wait()
    for i in range(cached // step):
        d = jnp.dot(pt_ref[chunk(i), :], dagg_ref[...], preferred_element_type=f32).astype(bf16)
        per = step // blk
        blocks = slice(i * per, (i + 1) * per)
        send_ref[blocks, :blk, :] = d.reshape(per, blk, width)
        copy = pltpu.make_async_copy(send_ref.at[blocks], send_hbm.at[blocks], send_sems.at[i])
        copy.start()
        leaving.append(copy)
    d = jnp.dot(pt_ref[cached:, :], dagg_ref[...], preferred_element_type=f32).astype(bf16)
    near_ref[...] = d.reshape(2, blk, width)
    for copy in leaving:
        copy.wait()


def per_device(
    features, stale, boundary, skip, tile_vals, tile_row, tile_src, tile_count, weight, cotangent
):
    feats = features[0]
    nodes, width = feats.shape
    parts = lax.axis_size(DOM)
    clusters = lax.axis_size("cluster")
    blk = stale.shape[1] // parts
    slots, _, tr = tile_vals.shape[1:]
    row_blocks = nodes // tr
    share = width // parts
    eights, fours = groups(clusters)
    odd = (lax.axis_index("cluster") % 2).astype(jnp.int32).reshape(1)
    start_row = boundary[0, 0] * blk
    own = lax.dynamic_slice_in_dim(feats, start_row, blk, 0)
    some = exchange(for_each(own, Z), eights).reshape(Z * blk, width)
    lower = passed_along(own, "cluster", 1)
    upper = passed_along(own, "cluster", -1)
    smem = pl.BlockSpec(memory_space=pltpu.SMEM)
    vmem = pl.BlockSpec(memory_space=pltpu.VMEM)
    hbm = pl.BlockSpec(memory_space=pltpu.HBM)
    base, p, pt = pl.pallas_call(
        before_kernel,
        out_shape=(
            jax.ShapeDtypeStruct((nodes, width), f32),
            jax.ShapeDtypeStruct((nodes, (parts + 4) * blk), bf16),
            jax.ShapeDtypeStruct(((parts + 2) * blk, nodes), bf16),
        ),
        in_specs=[smem] * 5 + [vmem] * 3,
        out_specs=(vmem,) * 3,
        scratch_shapes=[pltpu.VMEM((row_blocks, (2 * parts + 4) * blk, tr), f32)],
        compiler_params=pltpu.CompilerParams(vmem_limit_bytes=60 << 20),
        cost_estimate=pl.CostEstimate(
            flops=2 * nodes * width * parts * blk, bytes_accessed=8 << 20, transcendentals=0
        ),
        name="before",
    )(tile_src, tile_row, tile_count, skip, odd, tile_vals[0], feats, stale[0])
    table = exchange(for_each(some, YH), fours).reshape(parts * blk, width)
    out_features, dagg, send, near = pl.pallas_call(
        after_kernel,
        out_shape=(
            jax.ShapeDtypeStruct((nodes, width), bf16),
            jax.ShapeDtypeStruct((nodes, width), bf16),
            jax.ShapeDtypeStruct((parts, blk + share, width), bf16),
            jax.ShapeDtypeStruct((2, blk, width), bf16),
        ),
        in_specs=[smem] + [hbm] * 5 + [vmem] * 3,
        out_specs=(hbm, vmem, hbm, vmem),
        scratch_shapes=[
            pltpu.VMEM((nodes, width), f32),
            pltpu.VMEM((nodes, (parts + 4) * blk), bf16),
            pltpu.VMEM((nodes, width), bf16),
            pltpu.VMEM((width, width), bf16),
            pltpu.VMEM(((parts + 2) * blk, nodes), bf16),
            pltpu.VMEM((nodes, width), bf16),
            pltpu.VMEM((parts, blk + share, width), bf16),
            pltpu.VMEM((nodes, width), bf16),
            pltpu.VMEM((nodes, width), bf16),
            pltpu.SemaphoreType.DMA((nodes // 256 * 3 + 2,)),
            pltpu.SemaphoreType.DMA((nodes // 256,)),
            pltpu.SemaphoreType.DMA((parts * blk // 256,)),
        ],
        compiler_params=pltpu.CompilerParams(vmem_limit_bytes=48 << 20),
        cost_estimate=pl.CostEstimate(
            flops=2 * nodes * width * (3 * width + 2 * (parts + 1) * blk),
            bytes_accessed=11 << 20,
            transcendentals=nodes * width,
        ),
        name="after",
    )(odd, base, p, cotangent[0], weight, pt, table, lower, upper)
    rows = blk + share
    got = exchange(send.reshape(YH, Z * rows, width), fours)
    from_upper = passed_along(near[0], "cluster", -1)
    from_lower = passed_along(near[1], "cluster", 1)
    some = got.astype(f32).sum(axis=0).astype(bf16)
    some, from_upper, from_lower = lax.optimization_barrier((some, from_upper, from_lower))
    got = exchange(some.reshape(Z, rows, width), eights)
    mine = got.astype(f32).sum(axis=0)
    gw = lax.all_to_all(for_each(mine[blk:].astype(bf16), clusters), "cluster", 0, 0, tiled=True)
    grad_weight = gw.astype(f32).sum(axis=0)
    bgrad = mine[:blk] + from_upper.astype(f32) + from_lower.astype(f32)
    current = lax.dynamic_slice_in_dim(dagg, start_row, blk, 0).astype(f32)
    grad_features = lax.dynamic_update_slice_in_dim(
        dagg, (current + bgrad).astype(bf16), start_row, 0
    )
    return (out_features[None], grad_features[None], grad_weight)


def solution(mesh):
    finer = Mesh(mesh.devices.reshape(Z, YH, mesh.shape["cluster"]), ALL)
    placed = (
        P("cluster", DOM, None),
        P("cluster", None, None),
        P("cluster", DOM),
        P("cluster", None),
        P("cluster", DOM, None, None),
        P("cluster", DOM),
        P("cluster", DOM),
        P("cluster", DOM),
        P(),
        P("cluster", DOM, None),
    )
    return jax.shard_map(
        per_device,
        mesh=finer,
        in_specs=placed,
        out_specs=(P("cluster", DOM, None), P("cluster", DOM, None), P(DOM, None)),
        check_vma=False,
    )
```

```python
import jax
import jax.numpy as jnp
from jax import lax
from jax.experimental import pallas as pl
from jax.experimental.pallas import tpu as pltpu
from jax.sharding import Mesh
from jax.sharding import PartitionSpec as P

Z, YH = 8, 4
DOM = ("dom_0", "dom_1")
ALL = ("dom_0", "dom_1", "cluster")
f32 = jnp.float32
bf16 = jnp.bfloat16


def groups(clusters):
    at = lambda z, y, c: (z * YH + y) * clusters + c
    eights, fours = [], []
    for c in range(clusters):
        if c % 2 == 0:
            eights += [[at(z, y, c) for z in range(Z)] for y in range(YH)]
            fours += [[at(z, y, c) for y in range(YH)] for z in range(Z)]
        else:
            eights += [
                [at(2 * h + b, y, c) for b in range(2) for y in range(YH)] for h in range(Z // 2)
            ]
            fours += [
                [at(2 * h + b, y, c) for h in range(Z // 2)] for b in range(2) for y in range(YH)
            ]
    return eights, fours


def exchange(x, grouping):
    return lax.all_to_all(x, ALL, 0, 0, axis_index_groups=grouping, tiled=True)


def for_each(x, count):
    return jnp.broadcast_to(x, (count, *x.shape))


def passed_along(x, axis, by):
    count = lax.axis_size(axis)
    return lax.ppermute(x, axis, [(i, (i + by) % count) for i in range(count)])


def place_of(part, odd):
    return jnp.where(odd == 1, part, part % YH * Z + part // YH)


def before_kernel(
    src_ref, row_ref, count_ref, skip_ref, odd_ref, tiles_ref, feats_ref, stale_ref,
    base_ref, p_ref, pt_ref, acc_ref,
):
    slots, blk, tr = tiles_ref.shape
    parts = skip_ref.shape[1]
    cached = parts * blk
    acc_ref[...] = jnp.zeros_like(acc_ref)
    count = count_ref[0, 0]
    odd = odd_ref[0]

    def add_tile(t, carry):
        @pl.when(t < count)
        def _():
            s = src_ref[0, t]
            inside = jnp.minimum(s, parts - 1)
            kept = jnp.logical_and(s < parts, skip_ref[0, inside] == 1)
            sent = parts + jnp.where(s < parts, place_of(inside, odd), s)
            block = jnp.where(kept, s, sent)
            rows = pl.ds(pl.multiple_of(block * blk, blk), blk)
            r = row_ref[0, t]
            acc_ref[r, rows, :] += tiles_ref[t].astype(f32)

        return carry

    lax.fori_loop(0, slots, add_tile, 0)
    live = pt_ref.shape[0]
    for r in range(acc_ref.shape[0]):
        out = slice(r * tr, (r + 1) * tr)
        old = acc_ref[r, :cached, :].T.astype(bf16)
        base_ref[out, :] = feats_ref[out, :].astype(f32) + jnp.dot(
            old, stale_ref[...], preferred_element_type=f32
        )
        new = acc_ref[r, cached:, :]
        p_ref[out, :] = new.T.astype(bf16)
        pt_ref[:, out] = new[:live, :].astype(bf16)


def after_kernel(
    odd_ref, base_hbm, p_hbm, pt_hbm, cot_ref, weight_ref, table_ref, lower_ref, upper_ref,
    out_hbm, dagg_ref, send_ref, near_ref,
    base_ref, p_ref, pt_ref, out_ref, agg_ref, dz_ref, sems, out_sems,
):
    nodes, width = cot_ref.shape
    parts = send_ref.shape[0]
    blk = near_ref.shape[1]
    share = send_ref.shape[1] - blk
    step = 256
    steps = nodes // step
    chunk = lambda i: slice(i * step, (i + 1) * step)

    def fetch(source, target, rows, sem):
        copy = pltpu.make_async_copy(source.at[rows, :], target.at[rows, :], sems.at[sem])
        copy.start()
        return copy

    whole = slice(None)
    arriving = []
    for i in range(steps):
        rows = chunk(i)
        arriving.append(
            (fetch(p_hbm, p_ref, rows, 2 * i), fetch(base_hbm, base_ref, rows, 2 * i + 1))
        )
    of_pt = fetch(pt_hbm, pt_ref, whole, 2 * steps)
    cached = parts * blk
    near_rows = jnp.concatenate([lower_ref[...], upper_ref[...]], axis=0)
    leaving = []
    for i in range(steps):
        rows = chunk(i)
        of_p, of_base = arriving[i]
        if i == 0:
            of_p.wait()
            of_base.wait()
        if i == 1:
            for a, b in arriving[1:]:
                a.wait()
                b.wait()
            of_pt.wait()
        new = jnp.dot(p_ref[rows, :cached], table_ref[...], preferred_element_type=f32)
        new += jnp.dot(
            p_ref[rows, cached : cached + 2 * blk], near_rows, preferred_element_type=f32
        )
        agg = (base_ref[rows, :] + new).astype(bf16)
        agg_ref[rows, :] = agg
        z = jnp.dot(agg, weight_ref[...], preferred_element_type=f32)
        sig = jax.nn.sigmoid(z)
        out_ref[rows, :] = (z * sig).astype(bf16)
        copy = pltpu.make_async_copy(out_ref.at[rows, :], out_hbm.at[rows, :], out_sems.at[i])
        copy.start()
        leaving.append(copy)
        slope = sig * (1.0 + z * (1.0 - sig))
        dz = (cot_ref[rows, :].astype(f32) * slope).astype(bf16)
        dz_ref[rows, :] = dz
        dagg_ref[rows, :] = lax.dot_general(
            dz, weight_ref[...], (((1,), (1,)), ((), ())), preferred_element_type=f32
        ).astype(bf16)
    odd = odd_ref[0]
    for i in range(width // step):
        gw = lax.dot_general(
            agg_ref[:, chunk(i)], dz_ref[...], (((0,), (0,)), ((), ())), preferred_element_type=f32
        ).astype(bf16)
        per = step // share
        for j in range(per):
            place = place_of(jnp.int32(i * per + j), odd)
            send_ref[place, blk:, :] = gw[j * share : (j + 1) * share, :]
    for i in range(cached // step):
        d = jnp.dot(pt_ref[chunk(i), :], dagg_ref[...], preferred_element_type=f32).astype(bf16)
        per = step // blk
        blocks = slice(i * per, (i + 1) * per)
        send_ref[blocks, :blk, :] = d.reshape(per, blk, width)
    d = jnp.dot(pt_ref[cached:, :], dagg_ref[...], preferred_element_type=f32).astype(bf16)
    near_ref[...] = d.reshape(2, blk, width)
    for copy in leaving:
        copy.wait()


def last_kernel(got_ref, mine_ref, gw_ref):
    blk = mine_ref.shape[0]
    total = got_ref[0].astype(f32)
    for i in range(1, got_ref.shape[0]):
        total += got_ref[i].astype(f32)
    mine_ref[...] = total[:blk, :]
    gw_ref[...] = jnp.broadcast_to(total[blk:, :].astype(bf16)[None], gw_ref.shape)


def per_device(
    features, stale, boundary, skip, tile_vals, tile_row, tile_src, tile_count, weight, cotangent
):
    feats = features[0]
    nodes, width = feats.shape
    parts = lax.axis_size(DOM)
    clusters = lax.axis_size("cluster")
    blk = stale.shape[1] // parts
    slots, _, tr = tile_vals.shape[1:]
    row_blocks = nodes // tr
    share = width // parts
    eights, fours = groups(clusters)
    odd = (lax.axis_index("cluster") % 2).astype(jnp.int32).reshape(1)
    start_row = boundary[0, 0] * blk
    own = lax.dynamic_slice_in_dim(feats, start_row, blk, 0)
    some = exchange(for_each(own, Z), eights).reshape(Z * blk, width)
    lower = passed_along(own, "cluster", 1)
    upper = passed_along(own, "cluster", -1)
    smem = pl.BlockSpec(memory_space=pltpu.SMEM)
    vmem = pl.BlockSpec(memory_space=pltpu.VMEM)
    hbm = pl.BlockSpec(memory_space=pltpu.HBM)
    base, p, pt = pl.pallas_call(
        before_kernel,
        out_shape=(
            jax.ShapeDtypeStruct((nodes, width), f32),
            jax.ShapeDtypeStruct((nodes, (parts + 4) * blk), bf16),
            jax.ShapeDtypeStruct(((parts + 2) * blk, nodes), bf16),
        ),
        in_specs=[smem] * 5 + [vmem] * 3,
        out_specs=(vmem,) * 3,
        scratch_shapes=[pltpu.VMEM((row_blocks, (2 * parts + 4) * blk, tr), f32)],
        compiler_params=pltpu.CompilerParams(vmem_limit_bytes=60 << 20),
        cost_estimate=pl.CostEstimate(
            flops=2 * nodes * width * parts * blk, bytes_accessed=8 << 20, transcendentals=0
        ),
        name="before",
    )(tile_src, tile_row, tile_count, skip, odd, tile_vals[0], feats, stale[0])
    table = exchange(for_each(some, YH), fours).reshape(parts * blk, width)
    out_features, dagg, send, near = pl.pallas_call(
        after_kernel,
        out_shape=(
            jax.ShapeDtypeStruct((nodes, width), bf16),
            jax.ShapeDtypeStruct((nodes, width), bf16),
            jax.ShapeDtypeStruct((parts, blk + share, width), bf16),
            jax.ShapeDtypeStruct((2, blk, width), bf16),
        ),
        in_specs=[smem] + [hbm] * 3 + [vmem] * 5,
        out_specs=(hbm, vmem, vmem, vmem),
        scratch_shapes=[
            pltpu.VMEM((nodes, width), f32),
            pltpu.VMEM((nodes, (parts + 4) * blk), bf16),
            pltpu.VMEM(((parts + 2) * blk, nodes), bf16),
            pltpu.VMEM((nodes, width), bf16),
            pltpu.VMEM((nodes, width), bf16),
            pltpu.VMEM((nodes, width), bf16),
            pltpu.SemaphoreType.DMA((nodes // 256 * 2 + 1,)),
            pltpu.SemaphoreType.DMA((nodes // 256,)),
        ],
        compiler_params=pltpu.CompilerParams(vmem_limit_bytes=48 << 20),
        cost_estimate=pl.CostEstimate(
            flops=2 * nodes * width * (3 * width + 2 * (parts + 1) * blk),
            bytes_accessed=11 << 20,
            transcendentals=nodes * width,
        ),
        name="after",
    )(odd, base, p, pt, cotangent[0], weight, table, lower, upper)
    rows = blk + share
    got = exchange(send.reshape(YH, Z * rows, width), fours)
    got, near = lax.optimization_barrier((got, near))
    from_upper = passed_along(near[0], "cluster", -1)
    from_lower = passed_along(near[1], "cluster", 1)
    some = got.astype(f32).sum(axis=0).astype(bf16)
    got = exchange(some.reshape(Z, rows, width), eights)
    got, from_upper, from_lower = lax.optimization_barrier((got, from_upper, from_lower))
    mine, gw = pl.pallas_call(
        last_kernel,
        out_shape=(
            jax.ShapeDtypeStruct((blk, width), f32),
            jax.ShapeDtypeStruct((clusters, share, width), bf16),
        ),
        in_specs=[vmem],
        out_specs=(vmem, vmem),
        compiler_params=pltpu.CompilerParams(vmem_limit_bytes=8 << 20),
        name="last",
    )(got)
    gw = lax.all_to_all(gw, "cluster", 0, 0, tiled=True)
    grad_weight = gw.astype(f32).sum(axis=0)
    bgrad = mine + from_upper.astype(f32) + from_lower.astype(f32)
    current = lax.dynamic_slice_in_dim(dagg, start_row, blk, 0).astype(f32)
    grad_features = lax.dynamic_update_slice_in_dim(
        dagg, (current + bgrad).astype(bf16), start_row, 0
    )
    return (out_features[None], grad_features[None], grad_weight)


def solution(mesh):
    finer = Mesh(mesh.devices.reshape(Z, YH, mesh.shape["cluster"]), ALL)
    placed = (
        P("cluster", DOM, None),
        P("cluster", None, None),
        P("cluster", DOM),
        P("cluster", None),
        P("cluster", DOM, None, None),
        P("cluster", DOM),
        P("cluster", DOM),
        P("cluster", DOM),
        P(),
        P("cluster", DOM, None),
    )
    return jax.shard_map(
        per_device,
        mesh=finer,
        in_specs=placed,
        out_specs=(P("cluster", DOM, None), P("cluster", DOM, None), P(DOM, None)),
        check_vma=False,
    )
```

```python
import jax
import jax.numpy as jnp
from jax import lax
from jax.experimental import pallas as pl
from jax.experimental.pallas import tpu as pltpu
from jax.sharding import Mesh
from jax.sharding import PartitionSpec as P

Z, YH = 8, 4
DOM = ("dom_0", "dom_1")
ALL = ("dom_0", "dom_1", "cluster")
f32 = jnp.float32
bf16 = jnp.bfloat16


def groups(clusters):
    at = lambda z, y, c: (z * YH + y) * clusters + c
    eights, fours = [], []
    for c in range(clusters):
        if c % 2 == 0:
            eights += [[at(z, y, c) for z in range(Z)] for y in range(YH)]
            fours += [[at(z, y, c) for y in range(YH)] for z in range(Z)]
        else:
            eights += [
                [at(2 * h + b, y, c) for b in range(2) for y in range(YH)] for h in range(Z // 2)
            ]
            fours += [
                [at(2 * h + b, y, c) for h in range(Z // 2)] for b in range(2) for y in range(YH)
            ]
    return eights, fours


def exchange(x, grouping):
    return lax.all_to_all(x, ALL, 0, 0, axis_index_groups=grouping, tiled=True)


def for_each(x, count):
    return jnp.broadcast_to(x, (count, *x.shape))


def swapped(x, axis, first):
    count = lax.axis_size(axis)
    pairs = []
    for i in range(first, first + count, 2):
        a, b = i % count, (i + 1) % count
        pairs += [(a, b), (b, a)]
    return lax.ppermute(x, axis, pairs)


def place_of(part, odd):
    return jnp.where(odd == 1, part, part % YH * Z + part // YH)


def before_kernel(
    src_ref, row_ref, count_ref, skip_ref, odd_ref, tiles_ref, feats_ref, stale_ref,
    base_ref, p_ref, pt_ref, acc_ref,
):
    slots, blk, tr = tiles_ref.shape
    parts = skip_ref.shape[1]
    cached = parts * blk
    acc_ref[...] = jnp.zeros_like(acc_ref)
    count = count_ref[0, 0]
    odd = odd_ref[0]

    def add_tile(t, carry):
        @pl.when(t < count)
        def _():
            s = src_ref[0, t]
            inside = jnp.minimum(s, parts - 1)
            kept = jnp.logical_and(s < parts, skip_ref[0, inside] == 1)
            beside = jnp.where(odd == 1, s, 2 * parts + 1 - s)
            sent = parts + jnp.where(s < parts, place_of(inside, odd), beside)
            block = jnp.where(kept, s, sent)
            rows = pl.ds(pl.multiple_of(block * blk, blk), blk)
            r = row_ref[0, t]
            acc_ref[r, rows, :] += tiles_ref[t].astype(f32)

        return carry

    lax.fori_loop(0, slots, add_tile, 0)
    live = pt_ref.shape[0]
    for r in range(acc_ref.shape[0]):
        out = slice(r * tr, (r + 1) * tr)
        old = acc_ref[r, :cached, :].T.astype(bf16)
        base_ref[out, :] = feats_ref[out, :].astype(f32) + jnp.dot(
            old, stale_ref[...], preferred_element_type=f32
        )
        new = acc_ref[r, cached:, :]
        p_ref[out, :] = new.T.astype(bf16)
        pt_ref[:, out] = new[:live, :].astype(bf16)


def after_kernel(
    odd_ref, base_hbm, p_hbm, pt_hbm, cot_ref, weight_ref, table_ref, inner_ref, outer_ref,
    out_hbm, dagg_ref, send_ref, near_ref,
    base_ref, p_ref, pt_ref, out_ref, agg_ref, dz_ref, sems, out_sems,
):
    nodes, width = cot_ref.shape
    parts = send_ref.shape[0]
    blk = near_ref.shape[1]
    share = send_ref.shape[1] - blk
    step = 256
    steps = nodes // step
    chunk = lambda i: slice(i * step, (i + 1) * step)

    def fetch(source, target, rows, sem):
        copy = pltpu.make_async_copy(source.at[rows, :], target.at[rows, :], sems.at[sem])
        copy.start()
        return copy

    whole = slice(None)
    arriving = []
    for i in range(steps):
        rows = chunk(i)
        arriving.append(
            (fetch(p_hbm, p_ref, rows, 2 * i), fetch(base_hbm, base_ref, rows, 2 * i + 1))
        )
    of_pt = fetch(pt_hbm, pt_ref, whole, 2 * steps)
    cached = parts * blk
    near_rows = jnp.concatenate([inner_ref[...], outer_ref[...]], axis=0)
    leaving = []
    for i in range(steps):
        rows = chunk(i)
        of_p, of_base = arriving[i]
        if i == 0:
            of_p.wait()
            of_base.wait()
        if i == 1:
            for a, b in arriving[1:]:
                a.wait()
                b.wait()
            of_pt.wait()
        new = jnp.dot(p_ref[rows, :cached], table_ref[...], preferred_element_type=f32)
        new += jnp.dot(
            p_ref[rows, cached : cached + 2 * blk], near_rows, preferred_element_type=f32
        )
        agg = (base_ref[rows, :] + new).astype(bf16)
        agg_ref[rows, :] = agg
        z = jnp.dot(agg, weight_ref[...], preferred_element_type=f32)
        sig = jax.nn.sigmoid(z)
        out_ref[rows, :] = (z * sig).astype(bf16)
        copy = pltpu.make_async_copy(out_ref.at[rows, :], out_hbm.at[rows, :], out_sems.at[i])
        copy.start()
        leaving.append(copy)
        slope = sig * (1.0 + z * (1.0 - sig))
        dz = (cot_ref[rows, :].astype(f32) * slope).astype(bf16)
        dz_ref[rows, :] = dz
        dagg_ref[rows, :] = lax.dot_general(
            dz, weight_ref[...], (((1,), (1,)), ((), ())), preferred_element_type=f32
        ).astype(bf16)
    odd = odd_ref[0]
    for i in range(width // step):
        gw = lax.dot_general(
            agg_ref[:, chunk(i)], dz_ref[...], (((0,), (0,)), ((), ())), preferred_element_type=f32
        ).astype(bf16)
        per = step // share
        for j in range(per):
            place = place_of(jnp.int32(i * per + j), odd)
            send_ref[place, blk:, :] = gw[j * share : (j + 1) * share, :]
    for i in range(cached // step):
        d = jnp.dot(pt_ref[chunk(i), :], dagg_ref[...], preferred_element_type=f32).astype(bf16)
        per = step // blk
        blocks = slice(i * per, (i + 1) * per)
        send_ref[blocks, :blk, :] = d.reshape(per, blk, width)
    d = jnp.dot(pt_ref[cached:, :], dagg_ref[...], preferred_element_type=f32).astype(bf16)
    near_ref[...] = d.reshape(2, blk, width)
    for copy in leaving:
        copy.wait()


def last_kernel(got_ref, mine_ref, gw_ref):
    blk = mine_ref.shape[0]
    total = got_ref[0].astype(f32)
    for i in range(1, got_ref.shape[0]):
        total += got_ref[i].astype(f32)
    mine_ref[...] = total[:blk, :]
    gw_ref[...] = jnp.broadcast_to(total[blk:, :].astype(bf16)[None], gw_ref.shape)


def per_device(
    features, stale, boundary, skip, tile_vals, tile_row, tile_src, tile_count, weight, cotangent
):
    feats = features[0]
    nodes, width = feats.shape
    parts = lax.axis_size(DOM)
    clusters = lax.axis_size("cluster")
    blk = stale.shape[1] // parts
    slots, _, tr = tile_vals.shape[1:]
    row_blocks = nodes // tr
    share = width // parts
    eights, fours = groups(clusters)
    odd = (lax.axis_index("cluster") % 2).astype(jnp.int32).reshape(1)
    start_row = boundary[0, 0] * blk
    own = lax.dynamic_slice_in_dim(feats, start_row, blk, 0)
    some = exchange(for_each(own, Z), eights).reshape(Z * blk, width)
    inner = swapped(own, "cluster", 0)
    outer = swapped(own, "cluster", 1)
    smem = pl.BlockSpec(memory_space=pltpu.SMEM)
    vmem = pl.BlockSpec(memory_space=pltpu.VMEM)
    hbm = pl.BlockSpec(memory_space=pltpu.HBM)
    base, p, pt = pl.pallas_call(
        before_kernel,
        out_shape=(
            jax.ShapeDtypeStruct((nodes, width), f32),
            jax.ShapeDtypeStruct((nodes, (parts + 4) * blk), bf16),
            jax.ShapeDtypeStruct(((parts + 2) * blk, nodes), bf16),
        ),
        in_specs=[smem] * 5 + [vmem] * 3,
        out_specs=(vmem,) * 3,
        scratch_shapes=[pltpu.VMEM((row_blocks, (2 * parts + 4) * blk, tr), f32)],
        compiler_params=pltpu.CompilerParams(vmem_limit_bytes=60 << 20),
        cost_estimate=pl.CostEstimate(
            flops=2 * nodes * width * parts * blk, bytes_accessed=8 << 20, transcendentals=0
        ),
        name="before",
    )(tile_src, tile_row, tile_count, skip, odd, tile_vals[0], feats, stale[0])
    table = exchange(for_each(some, YH), fours).reshape(parts * blk, width)
    out_features, dagg, send, near = pl.pallas_call(
        after_kernel,
        out_shape=(
            jax.ShapeDtypeStruct((nodes, width), bf16),
            jax.ShapeDtypeStruct((nodes, width), bf16),
            jax.ShapeDtypeStruct((parts, blk + share, width), bf16),
            jax.ShapeDtypeStruct((2, blk, width), bf16),
        ),
        in_specs=[smem] + [hbm] * 3 + [vmem] * 5,
        out_specs=(hbm, vmem, vmem, vmem),
        scratch_shapes=[
            pltpu.VMEM((nodes, width), f32),
            pltpu.VMEM((nodes, (parts + 4) * blk), bf16),
            pltpu.VMEM(((parts + 2) * blk, nodes), bf16),
            pltpu.VMEM((nodes, width), bf16),
            pltpu.VMEM((nodes, width), bf16),
            pltpu.VMEM((nodes, width), bf16),
            pltpu.SemaphoreType.DMA((nodes // 256 * 2 + 1,)),
            pltpu.SemaphoreType.DMA((nodes // 256,)),
        ],
        compiler_params=pltpu.CompilerParams(vmem_limit_bytes=48 << 20),
        cost_estimate=pl.CostEstimate(
            flops=2 * nodes * width * (3 * width + 2 * (parts + 1) * blk),
            bytes_accessed=11 << 20,
            transcendentals=nodes * width,
        ),
        name="after",
    )(odd, base, p, pt, cotangent[0], weight, table, inner, outer)
    rows = blk + share
    got = exchange(send.reshape(YH, Z * rows, width), fours)
    got, near = lax.optimization_barrier((got, near))
    from_inner = swapped(near[0], "cluster", 0)
    from_outer = swapped(near[1], "cluster", 1)
    some = got.astype(f32).sum(axis=0).astype(bf16)
    got = exchange(some.reshape(Z, rows, width), eights)
    got, from_inner, from_outer = lax.optimization_barrier((got, from_inner, from_outer))
    mine, gw = pl.pallas_call(
        last_kernel,
        out_shape=(
            jax.ShapeDtypeStruct((blk, width), f32),
            jax.ShapeDtypeStruct((clusters, share, width), bf16),
        ),
        in_specs=[vmem],
        out_specs=(vmem, vmem),
        compiler_params=pltpu.CompilerParams(vmem_limit_bytes=8 << 20),
        name="last",
    )(got)
    gw = lax.all_to_all(gw, "cluster", 0, 0, tiled=True)
    grad_weight = gw.astype(f32).sum(axis=0)
    bgrad = mine + from_inner.astype(f32) + from_outer.astype(f32)
    current = lax.dynamic_slice_in_dim(dagg, start_row, blk, 0).astype(f32)
    grad_features = lax.dynamic_update_slice_in_dim(
        dagg, (current + bgrad).astype(bf16), start_row, 0
    )
    return (out_features[None], grad_features[None], grad_weight)


def solution(mesh):
    finer = Mesh(mesh.devices.reshape(Z, YH, mesh.shape["cluster"]), ALL)
    placed = (
        P("cluster", DOM, None),
        P("cluster", None, None),
        P("cluster", DOM),
        P("cluster", None),
        P("cluster", DOM, None, None),
        P("cluster", DOM),
        P("cluster", DOM),
        P("cluster", DOM),
        P(),
        P("cluster", DOM, None),
    )
    return jax.shard_map(
        per_device,
        mesh=finer,
        in_specs=placed,
        out_specs=(P("cluster", DOM, None), P("cluster", DOM, None), P(DOM, None)),
        check_vma=False,
    )
```

```python
import jax
import jax.numpy as jnp
from jax import lax
from jax.experimental import pallas as pl
from jax.experimental.pallas import tpu as pltpu
from jax.sharding import Mesh
from jax.sharding import PartitionSpec as P

Z, YH = 8, 4
DOM = ("dom_0", "dom_1")
ALL = ("dom_0", "dom_1", "cluster")
f32 = jnp.float32
bf16 = jnp.bfloat16


def groups(clusters):
    at = lambda z, y, c: (z * YH + y) * clusters + c
    eights, fours = [], []
    for c in range(clusters):
        if c % 2 == 0:
            eights += [[at(z, y, c) for z in range(Z)] for y in range(YH)]
            fours += [[at(z, y, c) for y in range(YH)] for z in range(Z)]
        else:
            eights += [
                [at(2 * h + b, y, c) for b in range(2) for y in range(YH)] for h in range(Z // 2)
            ]
            fours += [
                [at(2 * h + b, y, c) for h in range(Z // 2)] for b in range(2) for y in range(YH)
            ]
    return eights, fours


def exchange(x, grouping):
    return lax.all_to_all(x, ALL, 0, 0, axis_index_groups=grouping, tiled=True)


def for_each(x, count):
    return jnp.broadcast_to(x, (count, *x.shape))


def swapped(x, axis, first):
    count = lax.axis_size(axis)
    pairs = []
    for i in range(first, first + count, 2):
        a, b = i % count, (i + 1) % count
        pairs += [(a, b), (b, a)]
    return lax.ppermute(x, axis, pairs)


def place_of(part, odd):
    return jnp.where(odd == 1, part, part % YH * Z + part // YH)


def before_kernel(
    src_ref, row_ref, count_ref, skip_ref, odd_ref, tiles_ref, feats_ref, stale_ref,
    base_ref, p_ref, pt_ref, acc_ref,
):
    slots, blk, tr = tiles_ref.shape
    parts = skip_ref.shape[1]
    cached = parts * blk
    acc_ref[...] = jnp.zeros_like(acc_ref)
    count = count_ref[0, 0]
    odd = odd_ref[0]

    def add_tile(t, carry):
        @pl.when(t < count)
        def _():
            s = src_ref[0, t]
            inside = jnp.minimum(s, parts - 1)
            kept = jnp.logical_and(s < parts, skip_ref[0, inside] == 1)
            beside = jnp.where(odd == 1, s, 2 * parts + 1 - s)
            sent = parts + jnp.where(s < parts, place_of(inside, odd), beside)
            block = jnp.where(kept, s, sent)
            rows = pl.ds(pl.multiple_of(block * blk, blk), blk)
            r = row_ref[0, t]
            acc_ref[r, rows, :] += tiles_ref[t].astype(f32)

        return carry

    lax.fori_loop(0, slots, add_tile, 0)
    live = pt_ref.shape[0]
    for r in range(acc_ref.shape[0]):
        out = slice(r * tr, (r + 1) * tr)
        old = acc_ref[r, :cached, :].T.astype(bf16)
        base_ref[out, :] = feats_ref[out, :].astype(f32) + jnp.dot(
            old, stale_ref[...], preferred_element_type=f32
        )
        new = acc_ref[r, cached:, :]
        p_ref[out, :] = new.T.astype(bf16)
        pt_ref[:, out] = new[:live, :].astype(bf16)


def after_kernel(
    odd_ref, base_hbm, p_hbm, pt_hbm, cot_ref, weight_ref, table_ref, inner_ref, outer_ref,
    out_hbm, dagg_ref, send_ref, near_ref,
    base_ref, p_ref, pt_ref, out_ref, agg_ref, dz_ref, sems, out_sems,
):
    nodes, width = cot_ref.shape
    parts = send_ref.shape[0]
    blk = near_ref.shape[1]
    share = send_ref.shape[1] - blk
    step = 256
    steps = nodes // step
    chunk = lambda i: slice(i * step, (i + 1) * step)

    def fetch(source, target, rows, sem):
        copy = pltpu.make_async_copy(source.at[rows, :], target.at[rows, :], sems.at[sem])
        copy.start()
        return copy

    whole = slice(None)
    arriving = []
    for i in range(steps):
        rows = chunk(i)
        arriving.append(
            (fetch(p_hbm, p_ref, rows, 2 * i), fetch(base_hbm, base_ref, rows, 2 * i + 1))
        )
    of_pt = fetch(pt_hbm, pt_ref, whole, 2 * steps)
    cached = parts * blk
    near_rows = jnp.concatenate([inner_ref[...], outer_ref[...]], axis=0)
    leaving = []
    for i in range(steps):
        rows = chunk(i)
        of_p, of_base = arriving[i]
        if i == 0:
            of_p.wait()
            of_base.wait()
        if i == 1:
            for a, b in arriving[1:]:
                a.wait()
                b.wait()
            of_pt.wait()
        new = jnp.dot(p_ref[rows, :cached], table_ref[...], preferred_element_type=f32)
        new += jnp.dot(
            p_ref[rows, cached : cached + 2 * blk], near_rows, preferred_element_type=f32
        )
        agg = (base_ref[rows, :] + new).astype(bf16)
        agg_ref[rows, :] = agg
        z = jnp.dot(agg, weight_ref[...], preferred_element_type=f32)
        sig = jax.nn.sigmoid(z)
        out_ref[rows, :] = (z * sig).astype(bf16)
        copy = pltpu.make_async_copy(out_ref.at[rows, :], out_hbm.at[rows, :], out_sems.at[i])
        copy.start()
        leaving.append(copy)
        slope = sig * (1.0 + z * (1.0 - sig))
        dz = (cot_ref[rows, :].astype(f32) * slope).astype(bf16)
        dz_ref[rows, :] = dz
        dagg_ref[rows, :] = lax.dot_general(
            dz, weight_ref[...], (((1,), (1,)), ((), ())), preferred_element_type=f32
        ).astype(bf16)
    odd = odd_ref[0]
    for i in range(width // step):
        gw = lax.dot_general(
            agg_ref[:, chunk(i)], dz_ref[...], (((0,), (0,)), ((), ())), preferred_element_type=f32
        ).astype(bf16)
        per = step // share
        for j in range(per):
            place = place_of(jnp.int32(i * per + j), odd)
            send_ref[place, blk:, :] = gw[j * share : (j + 1) * share, :]
    for i in range(cached // step):
        d = jnp.dot(pt_ref[chunk(i), :], dagg_ref[...], preferred_element_type=f32).astype(bf16)
        per = step // blk
        blocks = slice(i * per, (i + 1) * per)
        send_ref[blocks, :blk, :] = d.reshape(per, blk, width)
    d = jnp.dot(pt_ref[cached:, :], dagg_ref[...], preferred_element_type=f32).astype(bf16)
    near_ref[...] = d.reshape(2, blk, width)
    for copy in leaving:
        copy.wait()


def last_kernel(got_ref, mine_ref, gw_ref):
    blk = mine_ref.shape[0]
    total = got_ref[0].astype(f32)
    for i in range(1, got_ref.shape[0]):
        total += got_ref[i].astype(f32)
    mine_ref[...] = total[:blk, :]
    gw_ref[...] = jnp.broadcast_to(total[blk:, :].astype(bf16)[None], gw_ref.shape)


def per_device(
    features, stale, boundary, skip, tile_vals, tile_row, tile_src, tile_count, weight, cotangent
):
    feats = features[0]
    nodes, width = feats.shape
    parts = lax.axis_size(DOM)
    clusters = lax.axis_size("cluster")
    blk = stale.shape[1] // parts
    slots, _, tr = tile_vals.shape[1:]
    row_blocks = nodes // tr
    share = width // parts
    eights, fours = groups(clusters)
    odd = (lax.axis_index("cluster") % 2).astype(jnp.int32).reshape(1)
    start_row = boundary[0, 0] * blk
    own = lax.dynamic_slice_in_dim(feats, start_row, blk, 0)
    some = exchange(for_each(own, Z), eights).reshape(Z * blk, width)
    inner = swapped(own, "cluster", 0)
    outer = swapped(own, "cluster", 1)
    some, inner, outer = lax.optimization_barrier((some, inner, outer))
    smem = pl.BlockSpec(memory_space=pltpu.SMEM)
    vmem = pl.BlockSpec(memory_space=pltpu.VMEM)
    hbm = pl.BlockSpec(memory_space=pltpu.HBM)
    base, p, pt = pl.pallas_call(
        before_kernel,
        out_shape=(
            jax.ShapeDtypeStruct((nodes, width), f32),
            jax.ShapeDtypeStruct((nodes, (parts + 4) * blk), bf16),
            jax.ShapeDtypeStruct(((parts + 2) * blk, nodes), bf16),
        ),
        in_specs=[smem] * 5 + [vmem] * 3,
        out_specs=(vmem,) * 3,
        scratch_shapes=[pltpu.VMEM((row_blocks, (2 * parts + 4) * blk, tr), f32)],
        compiler_params=pltpu.CompilerParams(vmem_limit_bytes=60 << 20),
        cost_estimate=pl.CostEstimate(
            flops=2 * nodes * width * parts * blk, bytes_accessed=8 << 20, transcendentals=0
        ),
        name="before",
    )(tile_src, tile_row, tile_count, skip, odd, tile_vals[0], feats, stale[0])
    table = exchange(for_each(some, YH), fours).reshape(parts * blk, width)
    out_features, dagg, send, near = pl.pallas_call(
        after_kernel,
        out_shape=(
            jax.ShapeDtypeStruct((nodes, width), bf16),
            jax.ShapeDtypeStruct((nodes, width), bf16),
            jax.ShapeDtypeStruct((parts, blk + share, width), bf16),
            jax.ShapeDtypeStruct((2, blk, width), bf16),
        ),
        in_specs=[smem] + [hbm] * 3 + [vmem] * 5,
        out_specs=(hbm, vmem, vmem, vmem),
        scratch_shapes=[
            pltpu.VMEM((nodes, width), f32),
            pltpu.VMEM((nodes, (parts + 4) * blk), bf16),
            pltpu.VMEM(((parts + 2) * blk, nodes), bf16),
            pltpu.VMEM((nodes, width), bf16),
            pltpu.VMEM((nodes, width), bf16),
            pltpu.VMEM((nodes, width), bf16),
            pltpu.SemaphoreType.DMA((nodes // 256 * 2 + 1,)),
            pltpu.SemaphoreType.DMA((nodes // 256,)),
        ],
        compiler_params=pltpu.CompilerParams(vmem_limit_bytes=48 << 20),
        cost_estimate=pl.CostEstimate(
            flops=2 * nodes * width * (3 * width + 2 * (parts + 1) * blk),
            bytes_accessed=11 << 20,
            transcendentals=nodes * width,
        ),
        name="after",
    )(odd, base, p, pt, cotangent[0], weight, table, inner, outer)
    rows = blk + share
    got = exchange(send.reshape(YH, Z * rows, width), fours)
    some = got.astype(f32).sum(axis=0).astype(bf16)
    got = exchange(some.reshape(Z, rows, width), eights)
    mine, gw = pl.pallas_call(
        last_kernel,
        out_shape=(
            jax.ShapeDtypeStruct((blk, width), f32),
            jax.ShapeDtypeStruct((clusters, share, width), bf16),
        ),
        in_specs=[vmem],
        out_specs=(vmem, vmem),
        compiler_params=pltpu.CompilerParams(vmem_limit_bytes=8 << 20),
        name="last",
    )(got)
    gw, near = lax.optimization_barrier((gw, near))
    gw = lax.all_to_all(gw, "cluster", 0, 0, tiled=True)
    from_inner = swapped(near[0], "cluster", 0)
    from_outer = swapped(near[1], "cluster", 1)
    grad_weight = gw.astype(f32).sum(axis=0)
    bgrad = mine + from_inner.astype(f32) + from_outer.astype(f32)
    current = lax.dynamic_slice_in_dim(dagg, start_row, blk, 0).astype(f32)
    grad_features = lax.dynamic_update_slice_in_dim(
        dagg, (current + bgrad).astype(bf16), start_row, 0
    )
    return (out_features[None], grad_features[None], grad_weight)


def solution(mesh):
    finer = Mesh(mesh.devices.reshape(Z, YH, mesh.shape["cluster"]), ALL)
    placed = (
        P("cluster", DOM, None),
        P("cluster", None, None),
        P("cluster", DOM),
        P("cluster", None),
        P("cluster", DOM, None, None),
        P("cluster", DOM),
        P("cluster", DOM),
        P("cluster", DOM),
        P(),
        P("cluster", DOM, None),
    )
    return jax.shard_map(
        per_device,
        mesh=finer,
        in_specs=placed,
        out_specs=(P("cluster", DOM, None), P("cluster", DOM, None), P(DOM, None)),
        check_vma=False,
    )
```

```python
import jax
import jax.numpy as jnp
from jax import lax
from jax.experimental import pallas as pl
from jax.experimental.pallas import tpu as pltpu
from jax.sharding import Mesh
from jax.sharding import PartitionSpec as P

Z, YH = 8, 4
DOM = ("dom_0", "dom_1")
ALL = ("dom_0", "dom_1", "cluster")
f32 = jnp.float32
bf16 = jnp.bfloat16


def groups(clusters):
    at = lambda z, y, c: (z * YH + y) * clusters + c
    eights, fours = [], []
    for c in range(clusters):
        if c % 2 == 0:
            eights += [[at(z, y, c) for z in range(Z)] for y in range(YH)]
            fours += [[at(z, y, c) for y in range(YH)] for z in range(Z)]
        else:
            eights += [
                [at(2 * h + b, y, c) for b in range(2) for y in range(YH)] for h in range(Z // 2)
            ]
            fours += [
                [at(2 * h + b, y, c) for h in range(Z // 2)] for b in range(2) for y in range(YH)
            ]
    return eights, fours


def exchange(x, grouping):
    return lax.all_to_all(x, ALL, 0, 0, axis_index_groups=grouping, tiled=True)


def for_each(x, count):
    return jnp.broadcast_to(x, (count, *x.shape))


def swapped(x, axis, first):
    count = lax.axis_size(axis)
    pairs = []
    for i in range(first, first + count, 2):
        a, b = i % count, (i + 1) % count
        pairs += [(a, b), (b, a)]
    return lax.ppermute(x, axis, pairs)


def place_of(part, odd):
    return jnp.where(odd == 1, part, part % YH * Z + part // YH)


def before_kernel(
    src_ref, row_ref, count_ref, skip_ref, odd_ref, tiles_ref, feats_ref, stale_ref,
    p_ref, pt_ref, acc_ref,
):
    slots, blk, tr = tiles_ref.shape
    parts = skip_ref.shape[1]
    cached = parts * blk
    acc_ref[...] = jnp.zeros_like(acc_ref)
    count = count_ref[0, 0]
    odd = odd_ref[0]

    def add_tile(t, carry):
        @pl.when(t < count)
        def _():
            s = src_ref[0, t]
            inside = jnp.minimum(s, parts - 1)
            kept = jnp.logical_and(s < parts, skip_ref[0, inside] == 1)
            beside = jnp.where(odd == 1, s, 2 * parts + 1 - s)
            sent = parts + jnp.where(s < parts, place_of(inside, odd), beside)
            block = jnp.where(kept, s, sent)
            rows = pl.ds(pl.multiple_of(block * blk, blk), blk)
            r = row_ref[0, t]
            acc_ref[r, rows, :] += tiles_ref[t].astype(f32)

        return carry

    lax.fori_loop(0, slots, add_tile, 0)
    live = pt_ref.shape[0]
    wide = acc_ref.shape[1] - cached
    for r in range(acc_ref.shape[0]):
        out = slice(r * tr, (r + 1) * tr)
        old = acc_ref[r, :cached, :].T.astype(bf16)
        base = feats_ref[out, :].astype(f32) + jnp.dot(
            old, stale_ref[...], preferred_element_type=f32
        )
        p_ref[out, wide:] = base.astype(bf16)
        new = acc_ref[r, cached:, :]
        p_ref[out, :wide] = new.T.astype(bf16)
        pt_ref[:, out] = new[:live, :].astype(bf16)


def after_kernel(
    odd_ref, p_hbm, pt_hbm, cot_ref, weight_ref, table_ref, inner_ref, outer_ref,
    out_hbm, dagg_ref, send_ref, near_ref,
    p_ref, pt_ref, out_ref, agg_ref, dz_ref, sems, out_sems,
):
    nodes, width = cot_ref.shape
    parts = send_ref.shape[0]
    blk = near_ref.shape[1]
    share = send_ref.shape[1] - blk
    step = 256
    steps = nodes // step
    chunk = lambda i: slice(i * step, (i + 1) * step)

    def fetch(source, target, rows, sem):
        copy = pltpu.make_async_copy(source.at[rows, :], target.at[rows, :], sems.at[sem])
        copy.start()
        return copy

    arriving = [fetch(p_hbm, p_ref, chunk(i), i) for i in range(steps)]
    of_pt = fetch(pt_hbm, pt_ref, slice(None), steps)
    cached = parts * blk
    wide = p_ref.shape[1] - width
    near_rows = jnp.concatenate([inner_ref[...], outer_ref[...]], axis=0)
    leaving = []
    for i in range(steps):
        rows = chunk(i)
        if i == 0:
            arriving[0].wait()
        if i == 1:
            for copy in arriving[1:]:
                copy.wait()
            of_pt.wait()
        new = jnp.dot(p_ref[rows, :cached], table_ref[...], preferred_element_type=f32)
        new += jnp.dot(
            p_ref[rows, cached : cached + 2 * blk], near_rows, preferred_element_type=f32
        )
        agg = (p_ref[rows, wide:].astype(f32) + new).astype(bf16)
        agg_ref[rows, :] = agg
        z = jnp.dot(agg, weight_ref[...], preferred_element_type=f32)
        sig = jax.nn.sigmoid(z)
        out_ref[rows, :] = (z * sig).astype(bf16)
        copy = pltpu.make_async_copy(out_ref.at[rows, :], out_hbm.at[rows, :], out_sems.at[i])
        copy.start()
        leaving.append(copy)
        slope = sig * (1.0 + z * (1.0 - sig))
        dz = (cot_ref[rows, :].astype(f32) * slope).astype(bf16)
        dz_ref[rows, :] = dz
        dagg_ref[rows, :] = lax.dot_general(
            dz, weight_ref[...], (((1,), (1,)), ((), ())), preferred_element_type=f32
        ).astype(bf16)
    odd = odd_ref[0]
    for i in range(width // step):
        gw = lax.dot_general(
            agg_ref[:, chunk(i)], dz_ref[...], (((0,), (0,)), ((), ())), preferred_element_type=f32
        ).astype(bf16)
        per = step // share
        for j in range(per):
            place = place_of(jnp.int32(i * per + j), odd)
            send_ref[place, blk:, :] = gw[j * share : (j + 1) * share, :]
    for i in range(cached // step):
        d = jnp.dot(pt_ref[chunk(i), :], dagg_ref[...], preferred_element_type=f32).astype(bf16)
        per = step // blk
        blocks = slice(i * per, (i + 1) * per)
        send_ref[blocks, :blk, :] = d.reshape(per, blk, width)
    d = jnp.dot(pt_ref[cached:, :], dagg_ref[...], preferred_element_type=f32).astype(bf16)
    near_ref[...] = d.reshape(2, blk, width)
    for copy in leaving:
        copy.wait()


def last_kernel(got_ref, mine_ref, gw_ref):
    blk = mine_ref.shape[0]
    total = got_ref[0].astype(f32)
    for i in range(1, got_ref.shape[0]):
        total += got_ref[i].astype(f32)
    mine_ref[...] = total[:blk, :]
    gw_ref[...] = jnp.broadcast_to(total[blk:, :].astype(bf16)[None], gw_ref.shape)


def per_device(
    features, stale, boundary, skip, tile_vals, tile_row, tile_src, tile_count, weight, cotangent
):
    feats = features[0]
    nodes, width = feats.shape
    parts = lax.axis_size(DOM)
    clusters = lax.axis_size("cluster")
    blk = stale.shape[1] // parts
    slots, _, tr = tile_vals.shape[1:]
    row_blocks = nodes // tr
    share = width // parts
    eights, fours = groups(clusters)
    odd = (lax.axis_index("cluster") % 2).astype(jnp.int32).reshape(1)
    start_row = boundary[0, 0] * blk
    own = lax.dynamic_slice_in_dim(feats, start_row, blk, 0)
    some = exchange(for_each(own, Z), eights).reshape(Z * blk, width)
    inner = swapped(own, "cluster", 0)
    outer = swapped(own, "cluster", 1)
    some, inner, outer = lax.optimization_barrier((some, inner, outer))
    smem = pl.BlockSpec(memory_space=pltpu.SMEM)
    vmem = pl.BlockSpec(memory_space=pltpu.VMEM)
    hbm = pl.BlockSpec(memory_space=pltpu.HBM)
    p, pt = pl.pallas_call(
        before_kernel,
        out_shape=(
            jax.ShapeDtypeStruct((nodes, (parts + 4) * blk + width), bf16),
            jax.ShapeDtypeStruct(((parts + 2) * blk, nodes), bf16),
        ),
        in_specs=[smem] * 5 + [vmem] * 3,
        out_specs=(vmem,) * 2,
        scratch_shapes=[pltpu.VMEM((row_blocks, (2 * parts + 4) * blk, tr), f32)],
        compiler_params=pltpu.CompilerParams(vmem_limit_bytes=60 << 20),
        cost_estimate=pl.CostEstimate(
            flops=2 * nodes * width * parts * blk, bytes_accessed=8 << 20, transcendentals=0
        ),
        name="before",
    )(tile_src, tile_row, tile_count, skip, odd, tile_vals[0], feats, stale[0])
    table = exchange(for_each(some, YH), fours).reshape(parts * blk, width)
    out_features, dagg, send, near = pl.pallas_call(
        after_kernel,
        out_shape=(
            jax.ShapeDtypeStruct((nodes, width), bf16),
            jax.ShapeDtypeStruct((nodes, width), bf16),
            jax.ShapeDtypeStruct((parts, blk + share, width), bf16),
            jax.ShapeDtypeStruct((2, blk, width), bf16),
        ),
        in_specs=[smem] + [hbm] * 2 + [vmem] * 5,
        out_specs=(hbm, vmem, vmem, vmem),
        scratch_shapes=[
            pltpu.VMEM((nodes, (parts + 4) * blk + width), bf16),
            pltpu.VMEM(((parts + 2) * blk, nodes), bf16),
            pltpu.VMEM((nodes, width), bf16),
            pltpu.VMEM((nodes, width), bf16),
            pltpu.VMEM((nodes, width), bf16),
            pltpu.SemaphoreType.DMA((nodes // 256 + 1,)),
            pltpu.SemaphoreType.DMA((nodes // 256,)),
        ],
        compiler_params=pltpu.CompilerParams(vmem_limit_bytes=48 << 20),
        cost_estimate=pl.CostEstimate(
            flops=2 * nodes * width * (3 * width + 2 * (parts + 1) * blk),
            bytes_accessed=11 << 20,
            transcendentals=nodes * width,
        ),
        name="after",
    )(odd, p, pt, cotangent[0], weight, table, inner, outer)
    rows = blk + share
    got = exchange(send.reshape(YH, Z * rows, width), fours)
    some = got.astype(f32).sum(axis=0).astype(bf16)
    got = exchange(some.reshape(Z, rows, width), eights)
    mine, gw = pl.pallas_call(
        last_kernel,
        out_shape=(
            jax.ShapeDtypeStruct((blk, width), f32),
            jax.ShapeDtypeStruct((clusters, share, width), bf16),
        ),
        in_specs=[vmem],
        out_specs=(vmem, vmem),
        compiler_params=pltpu.CompilerParams(vmem_limit_bytes=8 << 20),
        name="last",
    )(got)
    gw, near = lax.optimization_barrier((gw, near))
    gw = lax.all_to_all(gw, "cluster", 0, 0, tiled=True)
    from_outer = swapped(near[1], "cluster", 1)
    from_inner = swapped(near[0], "cluster", 0)
    grad_weight = gw.astype(f32).sum(axis=0)
    bgrad = mine + from_inner.astype(f32) + from_outer.astype(f32)
    current = lax.dynamic_slice_in_dim(dagg, start_row, blk, 0).astype(f32)
    grad_features = lax.dynamic_update_slice_in_dim(
        dagg, (current + bgrad).astype(bf16), start_row, 0
    )
    return (out_features[None], grad_features[None], grad_weight)


def solution(mesh):
    finer = Mesh(mesh.devices.reshape(Z, YH, mesh.shape["cluster"]), ALL)
    placed = (
        P("cluster", DOM, None),
        P("cluster", None, None),
        P("cluster", DOM),
        P("cluster", None),
        P("cluster", DOM, None, None),
        P("cluster", DOM),
        P("cluster", DOM),
        P("cluster", DOM),
        P(),
        P("cluster", DOM, None),
    )
    return jax.shard_map(
        per_device,
        mesh=finer,
        in_specs=placed,
        out_specs=(P("cluster", DOM, None), P("cluster", DOM, None), P(DOM, None)),
        check_vma=False,
    )
```

```python
import jax
import jax.numpy as jnp
from jax import lax
from jax.experimental import pallas as pl
from jax.experimental.pallas import tpu as pltpu
from jax.sharding import Mesh
from jax.sharding import PartitionSpec as P

Z, YH = 8, 4
DOM = ("dom_0", "dom_1")
ALL = ("dom_0", "dom_1", "cluster")
f32 = jnp.float32
bf16 = jnp.bfloat16


def groups(clusters):
    at = lambda z, y, c: (z * YH + y) * clusters + c
    eights, fours = [], []
    for c in range(clusters):
        if c % 2 == 1:
            eights += [[at(z, y, c) for z in range(Z)] for y in range(YH)]
            fours += [[at(z, y, c) for y in range(YH)] for z in range(Z)]
        else:
            eights += [
                [at(2 * h + b, y, c) for b in range(2) for y in range(YH)] for h in range(Z // 2)
            ]
            fours += [
                [at(2 * h + b, y, c) for h in range(Z // 2)] for b in range(2) for y in range(YH)
            ]
    return eights, fours


def exchange(x, grouping):
    return lax.all_to_all(x, ALL, 0, 0, axis_index_groups=grouping, tiled=True)


def for_each(x, count):
    return jnp.broadcast_to(x, (count, *x.shape))


def swapped(x, axis, first):
    count = lax.axis_size(axis)
    pairs = []
    for i in range(first, first + count, 2):
        a, b = i % count, (i + 1) % count
        pairs += [(a, b), (b, a)]
    return lax.ppermute(x, axis, pairs)


def place_of(part, odd):
    return jnp.where(odd == 0, part, part % YH * Z + part // YH)


def before_kernel(
    src_ref, row_ref, count_ref, skip_ref, odd_ref, tiles_ref, feats_ref, stale_ref,
    p_ref, pt_ref, acc_ref,
):
    slots, blk, tr = tiles_ref.shape
    parts = skip_ref.shape[1]
    cached = parts * blk
    acc_ref[...] = jnp.zeros_like(acc_ref)
    count = count_ref[0, 0]
    odd = odd_ref[0]

    def add_tile(t, carry):
        @pl.when(t < count)
        def _():
            s = src_ref[0, t]
            inside = jnp.minimum(s, parts - 1)
            kept = jnp.logical_and(s < parts, skip_ref[0, inside] == 1)
            beside = jnp.where(odd == 1, s, 2 * parts + 1 - s)
            sent = parts + jnp.where(s < parts, place_of(inside, odd), beside)
            block = jnp.where(kept, s, sent)
            rows = pl.ds(pl.multiple_of(block * blk, blk), blk)
            r = row_ref[0, t]
            acc_ref[r, rows, :] += tiles_ref[t].astype(f32)

        return carry

    lax.fori_loop(0, slots, add_tile, 0)
    live = pt_ref.shape[0]
    wide = acc_ref.shape[1] - cached
    for r in range(acc_ref.shape[0]):
        out = slice(r * tr, (r + 1) * tr)
        old = acc_ref[r, :cached, :].T.astype(bf16)
        base = feats_ref[out, :].astype(f32) + jnp.dot(
            old, stale_ref[...], preferred_element_type=f32
        )
        p_ref[out, wide:] = base.astype(bf16)
        new = acc_ref[r, cached:, :]
        p_ref[out, :wide] = new.T.astype(bf16)
        pt_ref[:, out] = new[:live, :].astype(bf16)


def after_kernel(
    odd_ref, p_hbm, pt_hbm, cot_ref, weight_ref, table_ref, inner_ref, outer_ref,
    out_hbm, dagg_ref, send_ref, near_ref,
    p_ref, pt_ref, out_ref, agg_ref, dz_ref, sems, out_sems,
):
    nodes, width = cot_ref.shape
    parts = send_ref.shape[0]
    blk = near_ref.shape[1]
    share = send_ref.shape[1] - blk
    step = 256
    steps = nodes // step
    chunk = lambda i: slice(i * step, (i + 1) * step)

    def fetch(source, target, rows, sem):
        copy = pltpu.make_async_copy(source.at[rows, :], target.at[rows, :], sems.at[sem])
        copy.start()
        return copy

    arriving = [fetch(p_hbm, p_ref, chunk(i), i) for i in range(steps)]
    of_pt = fetch(pt_hbm, pt_ref, slice(None), steps)
    cached = parts * blk
    wide = p_ref.shape[1] - width
    near_rows = jnp.concatenate([inner_ref[...], outer_ref[...]], axis=0)
    leaving = []
    for i in range(steps):
        rows = chunk(i)
        if i == 0:
            arriving[0].wait()
        if i == 1:
            for copy in arriving[1:]:
                copy.wait()
            of_pt.wait()
        new = jnp.dot(p_ref[rows, :cached], table_ref[...], preferred_element_type=f32)
        new += jnp.dot(
            p_ref[rows, cached : cached + 2 * blk], near_rows, preferred_element_type=f32
        )
        agg = (p_ref[rows, wide:].astype(f32) + new).astype(bf16)
        agg_ref[rows, :] = agg
        z = jnp.dot(agg, weight_ref[...], preferred_element_type=f32)
        sig = jax.nn.sigmoid(z)
        out_ref[rows, :] = (z * sig).astype(bf16)
        copy = pltpu.make_async_copy(out_ref.at[rows, :], out_hbm.at[rows, :], out_sems.at[i])
        copy.start()
        leaving.append(copy)
        slope = sig * (1.0 + z * (1.0 - sig))
        dz = (cot_ref[rows, :].astype(f32) * slope).astype(bf16)
        dz_ref[rows, :] = dz
        dagg_ref[rows, :] = lax.dot_general(
            dz, weight_ref[...], (((1,), (1,)), ((), ())), preferred_element_type=f32
        ).astype(bf16)
    odd = odd_ref[0]
    for i in range(width // step):
        gw = lax.dot_general(
            agg_ref[:, chunk(i)], dz_ref[...], (((0,), (0,)), ((), ())), preferred_element_type=f32
        ).astype(bf16)
        per = step // share
        for j in range(per):
            place = place_of(jnp.int32(i * per + j), odd)
            send_ref[place, blk:, :] = gw[j * share : (j + 1) * share, :]
    for i in range(cached // step):
        d = jnp.dot(pt_ref[chunk(i), :], dagg_ref[...], preferred_element_type=f32).astype(bf16)
        per = step // blk
        blocks = slice(i * per, (i + 1) * per)
        send_ref[blocks, :blk, :] = d.reshape(per, blk, width)
    d = jnp.dot(pt_ref[cached:, :], dagg_ref[...], preferred_element_type=f32).astype(bf16)
    near_ref[...] = d.reshape(2, blk, width)
    for copy in leaving:
        copy.wait()


def last_kernel(got_ref, mine_ref, gw_ref):
    blk = mine_ref.shape[0]
    total = got_ref[0].astype(f32)
    for i in range(1, got_ref.shape[0]):
        total += got_ref[i].astype(f32)
    mine_ref[...] = total[:blk, :]
    gw_ref[...] = jnp.broadcast_to(total[blk:, :].astype(bf16)[None], gw_ref.shape)


def per_device(
    features, stale, boundary, skip, tile_vals, tile_row, tile_src, tile_count, weight, cotangent
):
    feats = features[0]
    nodes, width = feats.shape
    parts = lax.axis_size(DOM)
    clusters = lax.axis_size("cluster")
    blk = stale.shape[1] // parts
    slots, _, tr = tile_vals.shape[1:]
    row_blocks = nodes // tr
    share = width // parts
    eights, fours = groups(clusters)
    odd = (lax.axis_index("cluster") % 2).astype(jnp.int32).reshape(1)
    start_row = boundary[0, 0] * blk
    own = lax.dynamic_slice_in_dim(feats, start_row, blk, 0)
    some = exchange(for_each(own, Z), eights).reshape(Z * blk, width)
    inner = swapped(own, "cluster", 0)
    outer = swapped(own, "cluster", 1)
    some, inner, outer = lax.optimization_barrier((some, inner, outer))
    smem = pl.BlockSpec(memory_space=pltpu.SMEM)
    vmem = pl.BlockSpec(memory_space=pltpu.VMEM)
    hbm = pl.BlockSpec(memory_space=pltpu.HBM)
    p, pt = pl.pallas_call(
        before_kernel,
        out_shape=(
            jax.ShapeDtypeStruct((nodes, (parts + 4) * blk + width), bf16),
            jax.ShapeDtypeStruct(((parts + 2) * blk, nodes), bf16),
        ),
        in_specs=[smem] * 5 + [vmem] * 3,
        out_specs=(vmem,) * 2,
        scratch_shapes=[pltpu.VMEM((row_blocks, (2 * parts + 4) * blk, tr), f32)],
        compiler_params=pltpu.CompilerParams(vmem_limit_bytes=60 << 20),
        cost_estimate=pl.CostEstimate(
            flops=2 * nodes * width * parts * blk, bytes_accessed=8 << 20, transcendentals=0
        ),
        name="before",
    )(tile_src, tile_row, tile_count, skip, odd, tile_vals[0], feats, stale[0])
    table = exchange(for_each(some, YH), fours).reshape(parts * blk, width)
    out_features, dagg, send, near = pl.pallas_call(
        after_kernel,
        out_shape=(
            jax.ShapeDtypeStruct((nodes, width), bf16),
            jax.ShapeDtypeStruct((nodes, width), bf16),
            jax.ShapeDtypeStruct((parts, blk + share, width), bf16),
            jax.ShapeDtypeStruct((2, blk, width), bf16),
        ),
        in_specs=[smem] + [hbm] * 2 + [vmem] * 5,
        out_specs=(hbm, vmem, vmem, vmem),
        scratch_shapes=[
            pltpu.VMEM((nodes, (parts + 4) * blk + width), bf16),
            pltpu.VMEM(((parts + 2) * blk, nodes), bf16),
            pltpu.VMEM((nodes, width), bf16),
            pltpu.VMEM((nodes, width), bf16),
            pltpu.VMEM((nodes, width), bf16),
            pltpu.SemaphoreType.DMA((nodes // 256 + 1,)),
            pltpu.SemaphoreType.DMA((nodes // 256,)),
        ],
        compiler_params=pltpu.CompilerParams(vmem_limit_bytes=48 << 20),
        cost_estimate=pl.CostEstimate(
            flops=2 * nodes * width * (3 * width + 2 * (parts + 1) * blk),
            bytes_accessed=11 << 20,
            transcendentals=nodes * width,
        ),
        name="after",
    )(odd, p, pt, cotangent[0], weight, table, inner, outer)
    rows = blk + share
    got = exchange(send.reshape(YH, Z * rows, width), fours)
    some = got.astype(f32).sum(axis=0).astype(bf16)
    got = exchange(some.reshape(Z, rows, width), eights)
    mine, gw = pl.pallas_call(
        last_kernel,
        out_shape=(
            jax.ShapeDtypeStruct((blk, width), f32),
            jax.ShapeDtypeStruct((clusters, share, width), bf16),
        ),
        in_specs=[vmem],
        out_specs=(vmem, vmem),
        compiler_params=pltpu.CompilerParams(vmem_limit_bytes=8 << 20),
        name="last",
    )(got)
    gw, near = lax.optimization_barrier((gw, near))
    gw = lax.all_to_all(gw, "cluster", 0, 0, tiled=True)
    from_outer = swapped(near[1], "cluster", 1)
    from_inner = swapped(near[0], "cluster", 0)
    grad_weight = gw.astype(f32).sum(axis=0)
    bgrad = mine + from_inner.astype(f32) + from_outer.astype(f32)
    current = lax.dynamic_slice_in_dim(dagg, start_row, blk, 0).astype(f32)
    grad_features = lax.dynamic_update_slice_in_dim(
        dagg, (current + bgrad).astype(bf16), start_row, 0
    )
    return (out_features[None], grad_features[None], grad_weight)


def solution(mesh):
    finer = Mesh(mesh.devices.reshape(Z, YH, mesh.shape["cluster"]), ALL)
    placed = (
        P("cluster", DOM, None),
        P("cluster", None, None),
        P("cluster", DOM),
        P("cluster", None),
        P("cluster", DOM, None, None),
        P("cluster", DOM),
        P("cluster", DOM),
        P("cluster", DOM),
        P(),
        P("cluster", DOM, None),
    )
    return jax.shard_map(
        per_device,
        mesh=finer,
        in_specs=placed,
        out_specs=(P("cluster", DOM, None), P("cluster", DOM, None), P(DOM, None)),
        check_vma=False,
    )
```
